128 devices in a mesh: ocean: 2 (over core), ice: 64 (over z, y, x).
Axes of the slice: x: 4, y: 4, z: 4, core: 2. Of those that a mesh axis runs over, the one named last changes fastest.
Arguments:
- velocity: float32 [128, 512, 128], P('ocean', 'ice'), may hold values from -6 to 6
- stress: float32 [128, 512, 128], P('ocean', 'ice'), may hold values from -6 to 6
- thickness: float32 [128, 512, 128], P('ocean', 'ice'), may hold values from 0.5 to 2
- forcing: float32 [128, 512, 128], P('ocean', 'ice'), may hold values from -6 to 6
- switch: int32 [128, 512, 128], P('ocean', 'ice'), may hold values 0 or 1
- covered: int32 [128], P('ocean'), may hold values from 0 to 1, as said below
- reinit: int32 [128], P('ocean'), may hold values 0 or 1
- cot_velocity: float32 [128, 512, 128], P('ocean', 'ice'), may hold values from -6 to 6
- cot_stress: float32 [128, 512, 128], P('ocean', 'ice'), may hold values from -6 to 6
- kernel: float32 [512, 512], replicated, may hold values from 0 to 1, as said below
Outputs:
- grad_velocity: float32 [128, 512, 128], P('ocean', 'ice')
- grad_stress: float32 [128, 512, 128], P('ocean', 'ice')
- grad_thickness: float32 [128, 512, 128], P('ocean', 'ice')
- grad_forcing: float32 [128, 512, 128], P('ocean', 'ice')
The draws below stay inside these ranges and needn't reach their ends.
Inputs may be any that keep to these rules, and one draw needn't show every extreme that they name: Exactly 32 blocks are covered; one index of ocean holds 31 of them and the other holds one. The kernel's diagonal exceeds the sum of each row's other entries.
All inputs are finite; a program needn't handle non-finite values. No bound on the sum of `switch` or of `reinit` on one device may be relied on, other than what follows from the above.
Results may differ from the reference program's by a relative error of at most 0.00015.
Values sent between devices are 32-bit elements; how exact they have to be, the bound alone decides.
No kernel may reach another device: no remote copies, remote signals or barrier semaphores. Data moves between devices by JAX's collectives and lax.ppermute only.
A program may use at most 64 MiB of HBM per device.

```python
import jax
import jax.numpy as jnp
from jax import lax

CELLS = 128
BLOCKS_DEV = 64
SUB = 8
WINDOWS = 2
ROWS = 512
BLOCKS = 128


def draw_covered(key, part):
    groups = BLOCKS // BLOCKS_DEV
    heavy = jax.random.randint(jax.random.fold_in(key, 11), (), 0, groups)
    pieces = []
    for group in range(groups):
        order = jax.random.permutation(jax.random.fold_in(key, 20 + group), BLOCKS_DEV)
        wanted = jnp.where(heavy == group, BLOCKS_DEV // 2 - 1, 1)
        pieces.append((order < wanted).astype(jnp.int32))
    return jnp.concatenate(pieces)


def draw_kernel(key, part):
    inner = jax.random.fold_in(key, 21)
    spread = jax.random.uniform(inner, (ROWS, ROWS), jnp.float32, 0.0, 0.8)
    return spread / ROWS + 0.6 * jnp.eye(ROWS, dtype=jnp.float32)


def set_ends(values, key, low, largest):
    index_at = [jax.random.randint(jax.random.fold_in(key, axis), (), 0, length) for axis, length in enumerate(values.shape)]
    longest = values.shape.index(max(values.shape))
    neighbour = index_at[:longest] + [(index_at[longest] + 1) % values.shape[longest]] + index_at[longest + 1:]
    return values.at[tuple(index_at)].set(low).at[tuple(neighbour)].set(largest)


def block_levels(stream_key, shape, shards, low, largest):
    def one(position, blocks):
        heights = jax.random.uniform(jax.random.fold_in(jax.random.fold_in(stream_key, 6), position), (blocks,), jnp.float32, low / len(shards), largest / len(shards))
        return jnp.repeat(jnp.exp(heights), shape[position] // blocks).reshape((-1,) + (1,) * (len(shape) - position - 1))

    gain = one(*shards[0])
    for cut in shards[1:]:
        gain = gain * one(*cut)
    return gain


def noise(rng, dims, deviation, reach, cuts=(), kind=jnp.bfloat16):
    array = jax.random.normal(rng, dims, jnp.float32) * deviation
    if len(cuts) > 0:
        array = block_levels(rng, dims, cuts, -0.22, 0.18) * array
    return jnp.clip(array, min=-reach, max=reach).astype(kind)


def setup_inputs(seed: int = 0) -> dict:
    key_of = jax.random.split(jax.random.key(seed), 11)
    velocity = noise(key_of[0], (BLOCKS, ROWS, CELLS), 1.0, 6.0, ((0, 2), (1, 64)), jnp.float32)
    stress = noise(key_of[1], (BLOCKS, ROWS, CELLS), 1.0, 6.0, ((0, 2), (1, 64)), jnp.float32)
    thickness = jnp.clip(0.5 + 1.5 * jax.random.uniform(key_of[2], (BLOCKS, ROWS, CELLS), jnp.float32) ** block_levels(key_of[2], (BLOCKS, ROWS, CELLS), ((0, 2), (1, 64)), -0.2, 0.2), 0.5, 2.0)
    forcing = noise(key_of[3], (BLOCKS, ROWS, CELLS), 1.0, 6.0, ((0, 2), (1, 64)), jnp.float32)
    switch = set_ends((jax.random.randint(key_of[4], (BLOCKS, ROWS, CELLS), 0, 2) < 1).astype(jnp.int32), jax.random.fold_in(key_of[4], 1), 0, 1)
    covered = draw_covered(jax.random.fold_in(key_of[10], 71), 0)
    reinit = set_ends((jax.random.randint(key_of[6], (BLOCKS,), 0, 2) < 1).astype(jnp.int32), jax.random.fold_in(key_of[6], 1), 0, 1)
    cot_velocity = noise(key_of[7], (BLOCKS, ROWS, CELLS), 1.0, 6.0, ((0, 2), (1, 64)), jnp.float32)
    cot_stress = noise(key_of[8], (BLOCKS, ROWS, CELLS), 1.0, 6.0, ((0, 2), (1, 64)), jnp.float32)
    kernel = draw_kernel(jax.random.fold_in(key_of[10], 71), 0)
    return dict(velocity=velocity, stress=stress, thickness=thickness, forcing=forcing, switch=switch, covered=covered, reinit=reinit, cot_velocity=cot_velocity, cot_stress=cot_stress, kernel=kernel)


PLASTIC = 0.25
VISCOUS = 1.0
GAMMA = 0.6
BETA = 0.9
STEP = 0.04

def forward_diff(x):
    upper = jnp.pad(x, ((0, 0), (1, 0), (0, 0)))[:, :-1]
    left = jnp.pad(x, ((0, 0), (0, 0), (1, 0)))[:, :, :-1]
    return 2.0 * x - upper - left

def backward_diff(x):
    lower = jnp.pad(x, ((0, 0), (0, 1), (0, 0)))[:, 1:]
    right = jnp.pad(x, ((0, 0), (0, 0), (0, 1)))[:, :, 1:]
    return 2.0 * x - lower - right

def evolve(velo, stress_now, source, force, keep, kernel):
    zeta = jnp.einsum('ij,bjc->bic', kernel, source, precision=lax.Precision.HIGHEST)
    u_now, s_now = (velo, stress_now)
    for window in range(WINDOWS):
        if window > 0:
            s_now = s_now * keep[:, None, None]
        for step in range(SUB):
            s_now = GAMMA * s_now + zeta * forward_diff(u_now)
            u_now = BETA * u_now - STEP * backward_diff(s_now) + STEP * force
    return (u_now, s_now)

def one_group(items):
    velo, stress_now, source, force, keep, kernel, cot_u, cot_s = items
    outputs, pullback = jax.vjp(lambda a, b, c, d: evolve(a, b, c, d, keep, kernel), velo, stress_now, source, force)
    return pullback((cot_u, cot_s))

def reference(velocity, stress, thickness, forcing, switch, covered, reinit, cot_velocity, cot_stress, kernel):
    coef = jnp.where(switch == 1, PLASTIC, VISCOUS).astype(jnp.float32)
    source = thickness * coef
    keep = (1 - reinit).astype(jnp.float32)
    groups = BLOCKS // BLOCKS_DEV

    def split(x):
        return x.reshape((groups, BLOCKS_DEV) + x.shape[1:])

    def mapped(items):
        velo, stress_now, src, force, kp, cot_u, cot_s = items
        return one_group((velo, stress_now, src, force, kp, kernel, cot_u, cot_s))
    gu, gs, gq, gf = lax.map(mapped, (split(velocity), split(stress), split(source), split(forcing), split(keep), split(cot_velocity), split(cot_stress)))
    live = covered.astype(jnp.float32)[:, None, None]
    shape = velocity.shape
    gu = gu.reshape(shape) * live
    gs = gs.reshape(shape) * live
    gq = gq.reshape(shape) * live
    gf = gf.reshape(shape) * live
    return (gu, gs, gq * coef, gf)
```

```python
import jax
import jax.numpy as jnp
from jax import lax
from jax.experimental import pallas as pl
from jax.experimental.pallas import tpu as pltpu
from jax.sharding import PartitionSpec as P

PLASTIC = 0.25
VISCOUS = 1.0
GAMMA = 0.6
BETA = 0.9
STEP = 0.04

HALF = 8
BLOCKS = 64
ICE = 64
SLOTS = 16
PARTS = 4
GROUPS = 64
ROWS = 512
F32 = jnp.float32
BF16 = jnp.bfloat16


def vmem():
    return pl.BlockSpec(memory_space=pltpu.VMEM)


def smem():
    return pl.BlockSpec(memory_space=pltpu.SMEM)


def ranked(covered_ref, index_ref):
    def clear(k, carry):
        index_ref[k] = 0
        return carry

    lax.fori_loop(0, BLOCKS, clear, 0)

    def visit(b, count):
        index_ref[count] = b
        return count + covered_ref[b]

    return lax.fori_loop(0, BLOCKS, visit, 0)


def gather_kernel(
    covered_ref, reinit_ref, velo_ref, stress_ref, thick_ref, switch_ref, force_ref, cotu_ref, cots_ref,
    own_ref, send_ref, keep_ref, index_ref,
):
    count = ranked(covered_ref, index_ref)
    heavy = count > 1

    def fields(block):
        coef = jnp.where(switch_ref[block] == 1, PLASTIC, VISCOUS)
        source = thick_ref[block] * coef
        return (velo_ref[block], cotu_ref[block], stress_ref[block], cots_ref[block], force_ref[block], source)

    def keep_row(block):
        return jnp.full((1, 128), 1 - reinit_ref[block], jnp.int32).astype(F32)

    def one_send(k, carry):
        block = index_ref[jnp.where(heavy, SLOTS + k, 0)]
        for f, tile in enumerate(fields(block)):
            send_ref[6 * k + f] = tile
        send_ref[6 * SLOTS + k, 0:1, :] = keep_row(block)
        return carry

    def one_own(k, carry):
        block = index_ref[jnp.where(heavy, k, 0)]
        for f, tile in enumerate(fields(block)):
            own_ref[6 * k + f] = tile
        keep_ref[k, 0:1, :] = keep_row(block)
        return carry

    lax.fori_loop(0, SLOTS - 1, one_send, 0)
    lax.fori_loop(0, SLOTS, one_own, 0)


def pack_kernel(covered_ref, own_ref, got_ref, keep_ref, out_ref, kept_ref):
    def add(b, count):
        return count + covered_ref[b]

    heavy = lax.fori_loop(0, BLOCKS, add, 0) > 1
    lane = lax.broadcasted_iota(jnp.int32, (8, 128), 1)
    low = lane < 64
    spot = lane % 64

    def one(k, carry):
        mine = jnp.logical_or(heavy, k == SLOTS - 1)
        tiles = [jnp.where(mine, own_ref[6 * k + f], got_ref[6 * k + f]) for f in range(6)]
        for q in range(PARTS):
            shift = (16 - 32 * q) % 128
            for t in range(3):
                both = jnp.where(
                    low,
                    pltpu.roll(tiles[2 * t], shift, 1) if shift else tiles[2 * t],
                    pltpu.roll(tiles[2 * t + 1], (shift + 64) % 128, 1),
                )
                if q == 0:
                    both = jnp.where(spot >= 16, both, 0.0)
                if q == PARTS - 1:
                    both = jnp.where(spot < 48, both, 0.0)
                out_ref[PARTS * k + q, pl.ds(8 * t, 8), :] = both
        return carry

    lax.fori_loop(0, SLOTS, one, 0)
    slot = lax.axis_index("ice") // PARTS
    mine = jnp.logical_or(heavy, slot == SLOTS - 1)
    row = jnp.where(mine, keep_ref[slot, 0:1, :], got_ref[6 * SLOTS + slot, 0:1, :])
    kept_ref[...] = jnp.broadcast_to(row, (8, 128))


def product(a, b, dims):
    a_high = a.astype(BF16)
    a_low = (a - a_high.astype(F32)).astype(BF16)
    b_high = b.astype(BF16)
    b_low = (b - b_high.astype(F32)).astype(BF16)

    def dot(x, y):
        return lax.dot_general(x, y, (dims, ((), ())), preferred_element_type=F32)

    return dot(a_low, b_high) + dot(a_high, b_low) + dot(a_high, b_high)


def spread(v):
    return pl.ds(v, 8, stride=GROUPS)


def work_kernel(
    in_ref, kernel_ref, kept_ref, out_ref,
    x_ref, y_ref, zf_ref, zb_ref, f_ref, acc_ref, af_ref, saved_ref, coef_ref, col_ref,
):
    part = lax.axis_index("ice") % PARTS
    lane = lax.broadcasted_iota(jnp.int32, (8, 128), 1)
    sub = lax.broadcasted_iota(jnp.int32, (8, 128), 0)
    low = lane < 64
    edge = jnp.logical_and(lane % 64 == 16, part == 0)

    last = in_ref[:, 16:24, :].reshape(ROWS, 128)
    col_ref[...] = product(kernel_ref[...], last, ((1,), (0,)))

    def load(v, t):
        return in_ref[pl.ds(v // 8, 8, stride=8), 8 * t + v % 8, :]

    for v in range(GROUPS):
        zeta = col_ref[spread(v), :]
        zb_ref[v] = jnp.where(low, -STEP, zeta)
        zf_ref[v] = jnp.where(low, pltpu.roll(zeta, 64, 1), -STEP)
        x_ref[v] = load(v, 0)
        y_ref[v] = load(v, 1)
        f_ref[v] = jnp.where(low, STEP * load(v, 2), 0.0)
        af_ref[v] = jnp.zeros((8, 128), F32)
        acc_ref[v] = jnp.zeros((8, 128), F32)

    gamma = jnp.full((8, 128), GAMMA, F32)
    for j in range(2 * HALF):
        coef_ref[j] = gamma
    coef_ref[0] = jnp.where(low, GAMMA, 1.0)
    coef_ref[HALF] = GAMMA * kept_ref[...]

    def subcycle(j, late):
        coef = coef_ref[j]
        above = jnp.where(sub == 0, 0.0, pltpu.roll(x_ref[GROUPS - 1], 1, 0))
        first_p = None
        held = None
        for v in range(GROUPS + 1):
            if v < GROUPS:
                x = x_ref[v]
                left = jnp.where(edge, 0.0, pltpu.roll(x, 1, 1))
                strain = (x + x) - above - left
                y = coef * y_ref[v] + zf_ref[v] * strain
                p = zb_ref[v] * y
                both = jnp.where(low, strain, y)
                if late:
                    acc_ref[v] += both * saved_ref[2 * HALF - 1 - j, v]
                else:
                    saved_ref[j, v] = pltpu.roll(both, 64, 1)
                y_ref[v] = y
                af_ref[v] += x
                above = x
                if v == 0:
                    first_p = p
                below = p
            else:
                below = jnp.where(sub == 7, 0.0, pltpu.roll(first_p, 7, 0))
            if v > 0:
                old_x, old_p = held
                right = pltpu.roll(old_p, 127, 1)
                x_ref[v - 1] = BETA * old_x + ((old_p + old_p) - below - right) + f_ref[v - 1]
            held = (x, p)

    def early(j, carry):
        subcycle(j, False)
        return carry

    def late(j, carry):
        subcycle(j, True)
        return carry

    lax.fori_loop(0, HALF, early, 0)
    lax.fori_loop(HALF, 2 * HALF, late, 0)

    for v in range(GROUPS):
        total = acc_ref[v]
        col_ref[spread(v), :] = total + pltpu.roll(total, 64, 1)
    adj_q = product(kernel_ref[...], col_ref[...], ((0,), (0,)))
    for v in range(GROUPS):
        tile = jnp.where(
            lane < 32,
            pltpu.roll(x_ref[v], 48, 1),
            jnp.where(lane < 64, GAMMA * pltpu.roll(y_ref[v], 80, 1), STEP * pltpu.roll(af_ref[v], 16, 1)),
        )
        col_ref[spread(v), :] = tile
    here = jnp.logical_and(lane >= 64, lane < 96)[None]
    moved = pltpu.roll(adj_q, 48, 1).reshape(GROUPS, 8, 128)
    result = jnp.where(here, moved, col_ref[...].reshape(GROUPS, 8, 128))
    out_ref[0] = result
    out_ref[1] = result


def unpack_kernel(covered_ref, back_ref, switch_ref, gu_ref, gs_ref, gq_ref, gf_ref, index_ref):
    count = ranked(covered_ref, index_ref)
    heavy = count > 1
    me = lax.axis_index("ocean")
    for ref in (gu_ref, gs_ref, gq_ref, gf_ref):
        ref[...] = jnp.zeros(ref.shape, F32)
    lane = lax.broadcasted_iota(jnp.int32, (8, 128), 1)
    outs = (gu_ref, gs_ref, gq_ref, gf_ref)

    def one(r, carry):
        block = index_ref[r]
        away = r >= SLOTS
        plane = jnp.where(away, 1 - me, me)
        slot = jnp.where(heavy, jnp.where(away, r - SLOTS, r), SLOTS - 1)
        base = plane * ICE + PARTS * slot
        tiles = [back_ref[base + q] for q in range(PARTS)]
        for f in range(4):
            whole = None
            for q in range(PARTS):
                shift = (32 * (q - f)) % 128
                moved = pltpu.roll(tiles[q], shift, 1) if shift else tiles[q]
                whole = moved if q == 0 else jnp.where(lane >= 32 * q, moved, whole)
            if f == 2:
                whole = whole * jnp.where(switch_ref[block] == 1, PLASTIC, VISCOUS)
            outs[f][block] = whole
        return carry

    lax.fori_loop(0, count, one, 0)


def shards(velocity, stress, thickness, forcing, switch, covered, reinit, cot_velocity, cot_stress, kernel):
    tile = (8, 128)

    def sds(*lead):
        return jax.ShapeDtypeStruct(lead + tile, F32)

    params = pltpu.CompilerParams(vmem_limit_bytes=48 * 1024 * 1024)
    own, send, keep = pl.pallas_call(
        gather_kernel,
        name="gather",
        out_shape=(sds(6 * SLOTS), sds(7 * SLOTS), sds(SLOTS)),
        in_specs=[smem(), smem()] + [vmem()] * 7,
        out_specs=(vmem(), vmem(), vmem()),
        scratch_shapes=[pltpu.SMEM((BLOCKS,), jnp.int32)],
        compiler_params=params,
    )(covered, reinit, velocity, stress, thickness, switch, forcing, cot_velocity, cot_stress)
    got = lax.ppermute(send, "ocean", [(0, 1), (1, 0)])
    packed, kept = pl.pallas_call(
        pack_kernel,
        name="pack",
        out_shape=(jax.ShapeDtypeStruct((ICE, 24, 128), F32), sds()),
        in_specs=[smem()] + [vmem()] * 3,
        out_specs=(vmem(), vmem()),
        compiler_params=params,
    )(covered, own, got, keep)
    arrived = lax.all_to_all(packed, "ice", split_axis=0, concat_axis=0, tiled=True)
    col = pltpu.VMEM((GROUPS,) + tile, F32)
    result = pl.pallas_call(
        work_kernel,
        name="work",
        out_shape=sds(2, ICE),
        in_specs=[vmem()] * 3,
        out_specs=vmem(),
        scratch_shapes=[col] * 7
        + [
            pltpu.VMEM((HALF, GROUPS) + tile, F32),
            pltpu.VMEM((2 * HALF,) + tile, F32),
            pltpu.VMEM((ROWS, 128), F32),
        ],
        compiler_params=params,
    )(arrived, kernel, kept)
    back = lax.all_to_all(result.reshape(2 * ICE, 8, 128), ("ocean", "ice"), split_axis=0, concat_axis=0, tiled=True)
    return pl.pallas_call(
        unpack_kernel,
        name="unpack",
        out_shape=(sds(BLOCKS),) * 4,
        in_specs=[smem(), vmem(), vmem()],
        out_specs=(vmem(),) * 4,
        scratch_shapes=[pltpu.SMEM((BLOCKS,), jnp.int32)],
        compiler_params=params,
    )(covered, back, switch)


def solution(mesh):
    cells = P("ocean", "ice", None)
    return jax.shard_map(
        shards,
        mesh=mesh,
        in_specs=(cells, cells, cells, cells, cells, P("ocean"), P("ocean"), cells, cells, P()),
        out_specs=(cells, cells, cells, cells),
        check_vma=False,
    )
```

```python
import jax
import jax.numpy as jnp
from jax import lax
from jax.experimental import pallas as pl
from jax.experimental.pallas import tpu as pltpu
from jax.sharding import PartitionSpec as P

PLASTIC = 0.25
VISCOUS = 1.0
GAMMA = 0.6
BETA = 0.9
STEP = 0.04

HALF = 8
BLOCKS = 64
ICE = 64
SLOTS = 16
PARTS = 4
GROUPS = 64
ROWS = 512
MOST = 31
F32 = jnp.float32
BF16 = jnp.bfloat16


def vmem():
    return pl.BlockSpec(memory_space=pltpu.VMEM)


def smem():
    return pl.BlockSpec(memory_space=pltpu.SMEM)


def ranked(covered_ref, index_ref, empty):
    for k in range(MOST + 1):
        index_ref[k] = empty
    count = jnp.int32(0)
    for b in range(BLOCKS):
        flag = covered_ref[b]
        index_ref[jnp.where(flag == 1, count, MOST)] = b
        count = count + flag
    return count


def is_heavy(covered_ref):
    count = covered_ref[0]
    for b in range(1, BLOCKS):
        count = count + covered_ref[b]
    return count > 1


def gather_kernel(
    covered_hbm, reinit_hbm, velo_hbm, cotu_hbm, stress_hbm, cots_hbm, force_hbm, thick_hbm, switch_hbm,
    own_ref, send_ref, keep_ref,
    covered_ref, reinit_ref, velo_ref, cotu_ref, stress_ref, cots_ref, force_ref, thick_ref, switch_ref,
    index_ref, sems,
):
    sources = (covered_hbm, reinit_hbm, velo_hbm, cotu_hbm, stress_hbm, cots_hbm, force_hbm, thick_hbm, switch_hbm)
    targets = (covered_ref, reinit_ref, velo_ref, cotu_ref, stress_ref, cots_ref, force_ref, thick_ref, switch_ref)
    copies = [pltpu.make_async_copy(a, b, sems.at[i]) for i, (a, b) in enumerate(zip(sources, targets))]
    for copy in copies:
        copy.start()
    copies[0].wait()
    heavy = ranked(covered_ref, index_ref, 0) > 1
    for copy in copies[1:]:
        copy.wait()

    def put(block, k, out_ref):
        coef = jnp.where(switch_ref[block] == 1, PLASTIC, VISCOUS)
        out_ref[6 * k] = velo_ref[block]
        out_ref[6 * k + 1] = cotu_ref[block]
        out_ref[6 * k + 2] = stress_ref[block]
        out_ref[6 * k + 3] = cots_ref[block]
        out_ref[6 * k + 4] = force_ref[block]
        out_ref[6 * k + 5] = thick_ref[block] * coef
        return jnp.full((1, 128), 1 - reinit_ref[block], jnp.int32).astype(F32)

    for k in range(SLOTS - 1):
        block = index_ref[jnp.where(heavy, SLOTS + k, 0)]
        send_ref[6 * SLOTS + k // 8, k % 8 : k % 8 + 1, :] = put(block, k, send_ref)
    for k in range(SLOTS):
        block = index_ref[jnp.where(heavy, k, 0)]
        keep_ref[k // 8, k % 8 : k % 8 + 1, :] = put(block, k, own_ref)


def pack_kernel(covered_ref, own_ref, got_ref, keep_ref, out_ref, kept_ref):
    heavy = is_heavy(covered_ref)
    lane = lax.broadcasted_iota(jnp.int32, (8, 128), 1)
    low = lane < 64
    spot = lane % 64

    for k in range(SLOTS):
        tiles = [own_ref[6 * k + f] for f in range(6)]
        if k < SLOTS - 1:
            tiles = [jnp.where(heavy, tile, got_ref[6 * k + f]) for f, tile in enumerate(tiles)]
        for q in range(PARTS):
            shift = (16 - 32 * q) % 128
            for t in range(3):
                both = jnp.where(
                    low,
                    pltpu.roll(tiles[2 * t], shift, 1) if shift else tiles[2 * t],
                    pltpu.roll(tiles[2 * t + 1], (shift + 64) % 128, 1),
                )
                if q == 0:
                    both = jnp.where(spot >= 16, both, 0.0)
                if q == PARTS - 1:
                    both = jnp.where(spot < 48, both, 0.0)
                out_ref[PARTS * k + q, pl.ds(8 * t, 8), :] = both
    slot = lax.axis_index("ice") // PARTS
    mine = jnp.logical_or(heavy, slot == SLOTS - 1)
    sub = slot % 8
    row = jnp.where(
        mine, keep_ref[slot // 8, pl.ds(sub, 1), :], got_ref[6 * SLOTS + slot // 8, pl.ds(sub, 1), :]
    )
    kept_ref[...] = jnp.broadcast_to(row, (8, 128))


def product(a, b, dims):
    a_high = a.astype(BF16)
    a_low = (a - a_high.astype(F32)).astype(BF16)
    b_high = b.astype(BF16)
    b_low = (b - b_high.astype(F32)).astype(BF16)

    def dot(x, y):
        return lax.dot_general(x, y, (dims, ((), ())), preferred_element_type=F32)

    return dot(a_low, b_high) + dot(a_high, b_low) + dot(a_high, b_high)


def spread(v):
    return pl.ds(v, 8, stride=GROUPS)


def work_kernel(
    in_ref, kernel_ref, kept_ref, out_ref,
    x_ref, y_ref, zf_ref, zb_ref, f_ref, acc_ref, af_ref, saved_ref, coef_ref, col_ref,
):
    part = lax.axis_index("ice") % PARTS
    lane = lax.broadcasted_iota(jnp.int32, (8, 128), 1)
    sub = lax.broadcasted_iota(jnp.int32, (8, 128), 0)
    low = lane < 64
    edge = jnp.logical_and(lane % 64 == 16, part == 0)

    last = in_ref[:, 16:24, :].reshape(ROWS, 128)
    col_ref[...] = product(kernel_ref[...], last, ((1,), (0,)))

    def load(v, t):
        return in_ref[pl.ds(v // 8, 8, stride=8), 8 * t + v % 8, :]

    for v in range(GROUPS):
        zeta = col_ref[spread(v), :]
        zb_ref[v] = jnp.where(low, -STEP, zeta)
        zf_ref[v] = jnp.where(low, pltpu.roll(zeta, 64, 1), -STEP)
        x_ref[v] = load(v, 0)
        y_ref[v] = load(v, 1)
        f_ref[v] = jnp.where(low, STEP * load(v, 2), 0.0)
        af_ref[v] = jnp.zeros((8, 128), F32)
        acc_ref[v] = jnp.zeros((8, 128), F32)

    gamma = jnp.full((8, 128), GAMMA, F32)
    for j in range(2 * HALF):
        coef_ref[j] = gamma
    coef_ref[0] = jnp.where(low, GAMMA, 1.0)
    coef_ref[HALF] = GAMMA * kept_ref[...]

    def subcycle(j, late):
        coef = coef_ref[j]
        above = jnp.where(sub == 0, 0.0, pltpu.roll(x_ref[GROUPS - 1], 1, 0))
        first_p = None
        held = None
        for v in range(GROUPS + 1):
            if v < GROUPS:
                x = x_ref[v]
                left = jnp.where(edge, 0.0, pltpu.roll(x, 1, 1))
                strain = (x + x) - above - left
                y = coef * y_ref[v] + zf_ref[v] * strain
                p = zb_ref[v] * y
                both = jnp.where(low, strain, y)
                if late:
                    acc_ref[v] += both * saved_ref[2 * HALF - 1 - j, v]
                else:
                    saved_ref[j, v] = pltpu.roll(both, 64, 1)
                y_ref[v] = y
                af_ref[v] += x
                above = x
                if v == 0:
                    first_p = p
                below = p
            else:
                below = jnp.where(sub == 7, 0.0, pltpu.roll(first_p, 7, 0))
            if v > 0:
                old_x, old_p = held
                right = pltpu.roll(old_p, 127, 1)
                x_ref[v - 1] = BETA * old_x + ((old_p + old_p) - below - right) + f_ref[v - 1]
            held = (x, p)

    for j in range(2 * HALF):
        subcycle(j, j >= HALF)

    for v in range(GROUPS):
        total = acc_ref[v]
        col_ref[spread(v), :] = total + pltpu.roll(total, 64, 1)
    adj_q = product(kernel_ref[...], col_ref[...], ((0,), (0,)))
    for v in range(GROUPS):
        tile = jnp.where(
            lane < 32,
            pltpu.roll(x_ref[v], 48, 1),
            jnp.where(lane < 64, GAMMA * pltpu.roll(y_ref[v], 80, 1), STEP * pltpu.roll(af_ref[v], 16, 1)),
        )
        col_ref[spread(v), :] = tile
    here = jnp.logical_and(lane >= 64, lane < 96)[None]
    moved = pltpu.roll(adj_q, 48, 1).reshape(GROUPS, 8, 128)
    result = jnp.where(here, moved, col_ref[...].reshape(GROUPS, 8, 128))
    out_ref[0] = result
    out_ref[1] = result


def unpack_kernel(covered_ref, back_ref, switch_ref, gu_hbm, gs_hbm, gq_hbm, gf_hbm, all_ref, index_ref, sems):
    heavy = ranked(covered_ref, index_ref, BLOCKS) > 1
    me = lax.axis_index("ocean")
    all_ref[...] = jnp.zeros(all_ref.shape, F32)
    lane = lax.broadcasted_iota(jnp.int32, (8, 128), 1)
    for r in range(MOST):
        block = index_ref[r]
        if r >= SLOTS:
            base = (1 - me) * ICE + PARTS * (r - SLOTS)
        else:
            base = me * ICE + jnp.where(heavy, PARTS * r, PARTS * (SLOTS - 1))
        tiles = [back_ref[base + q] for q in range(PARTS)]
        for f in range(4):
            whole = None
            for q in range(PARTS):
                shift = (32 * (q - f)) % 128
                moved = pltpu.roll(tiles[q], shift, 1) if shift else tiles[q]
                whole = moved if q == 0 else jnp.where(lane >= 32 * q, moved, whole)
            if f == 2:
                inside = jnp.minimum(block, BLOCKS - 1)
                whole = whole * jnp.where(switch_ref[inside] == 1, PLASTIC, VISCOUS)
            all_ref[f, block] = whole
    copies = []
    for f, ref in enumerate((gu_hbm, gs_hbm, gq_hbm, gf_hbm)):
        for part in range(2):
            rows = pl.ds(part * (BLOCKS // 2), BLOCKS // 2)
            copies.append(pltpu.make_async_copy(all_ref.at[f, rows], ref.at[rows], sems.at[2 * f + part]))
    for copy in copies:
        copy.start()
    for copy in copies:
        copy.wait()


def shards(velocity, stress, thickness, forcing, switch, covered, reinit, cot_velocity, cot_stress, kernel):
    tile = (8, 128)

    def sds(*lead):
        return jax.ShapeDtypeStruct(lead + tile, F32)

    params = pltpu.CompilerParams(vmem_limit_bytes=48 * 1024 * 1024)
    own, send, keep = pl.pallas_call(
        gather_kernel,
        name="gather",
        out_shape=(sds(6 * SLOTS), sds(6 * SLOTS + 2), sds(2)),
        in_specs=[pl.BlockSpec(memory_space=pl.ANY)] * 9,
        out_specs=(vmem(), vmem(), vmem()),
        scratch_shapes=[pltpu.SMEM((BLOCKS,), jnp.int32)] * 2
        + [pltpu.VMEM((BLOCKS,) + tile, F32)] * 6
        + [pltpu.VMEM((BLOCKS,) + tile, jnp.int32), pltpu.SMEM((MOST + 1,), jnp.int32), pltpu.SemaphoreType.DMA((9,))],
        compiler_params=params,
    )(covered, reinit, velocity, cot_velocity, stress, cot_stress, forcing, thickness, switch)
    got = lax.ppermute(send, "ocean", [(0, 1), (1, 0)])
    packed, kept = pl.pallas_call(
        pack_kernel,
        name="pack",
        out_shape=(jax.ShapeDtypeStruct((ICE, 24, 128), F32), sds()),
        in_specs=[smem()] + [vmem()] * 3,
        out_specs=(vmem(), vmem()),
        compiler_params=params,
    )(covered, own, got, keep)
    arrived = lax.all_to_all(packed, "ice", split_axis=0, concat_axis=0, tiled=True)
    col = pltpu.VMEM((GROUPS,) + tile, F32)
    result = pl.pallas_call(
        work_kernel,
        name="work",
        out_shape=sds(2, ICE),
        in_specs=[vmem()] * 3,
        out_specs=vmem(),
        scratch_shapes=[col] * 7
        + [
            pltpu.VMEM((HALF, GROUPS) + tile, F32),
            pltpu.VMEM((2 * HALF,) + tile, F32),
            pltpu.VMEM((ROWS, 128), F32),
        ],
        compiler_params=params,
    )(arrived, kernel, kept)
    back = lax.all_to_all(result.reshape(2 * ICE, 8, 128), ("ocean", "ice"), split_axis=0, concat_axis=0, tiled=True)
    return pl.pallas_call(
        unpack_kernel,
        name="unpack",
        out_shape=(sds(BLOCKS),) * 4,
        in_specs=[smem(), vmem(), vmem()],
        out_specs=(pl.BlockSpec(memory_space=pl.ANY),) * 4,
        scratch_shapes=[
            pltpu.VMEM((4, BLOCKS + 1) + tile, F32),
            pltpu.SMEM((MOST + 1,), jnp.int32),
            pltpu.SemaphoreType.DMA((8,)),
        ],
        compiler_params=params,
    )(covered, back, switch)


def solution(mesh):
    cells = P("ocean", "ice", None)
    return jax.shard_map(
        shards,
        mesh=mesh,
        in_specs=(cells, cells, cells, cells, cells, P("ocean"), P("ocean"), cells, cells, P()),
        out_specs=(cells, cells, cells, cells),
        check_vma=False,
    )
```

```python
import jax
import jax.numpy as jnp
from jax import lax
from jax.experimental import pallas as pl
from jax.experimental.pallas import tpu as pltpu
from jax.sharding import PartitionSpec as P

PLASTIC = 0.25
VISCOUS = 1.0
GAMMA = 0.6
BETA = 0.9
STEP = 0.04

HALF = 8
BLOCKS = 64
ICE = 64
SLOTS = 16
PARTS = 4
GROUPS = 64
ROWS = 512
MOST = 31
F32 = jnp.float32
BF16 = jnp.bfloat16


def vmem():
    return pl.BlockSpec(memory_space=pltpu.VMEM)


def smem():
    return pl.BlockSpec(memory_space=pltpu.SMEM)


def ranked(covered_ref, index_ref, empty):
    for k in range(MOST + 1):
        index_ref[k] = empty
    count = jnp.int32(0)
    for b in range(BLOCKS):
        flag = covered_ref[b]
        index_ref[jnp.where(flag == 1, count, MOST)] = b
        count = count + flag
    return count


def is_heavy(covered_ref):
    count = covered_ref[0]
    for b in range(1, BLOCKS):
        count = count + covered_ref[b]
    return count > 1


def gather_kernel(
    covered_hbm, reinit_hbm, velo_hbm, cotu_hbm, stress_hbm, cots_hbm, force_hbm, thick_hbm, switch_hbm,
    own_ref, send_ref, keep_ref,
    covered_ref, reinit_ref, velo_ref, cotu_ref, stress_ref, cots_ref, force_ref, thick_ref, switch_ref,
    index_ref, sems,
):
    sources = (covered_hbm, reinit_hbm, velo_hbm, cotu_hbm, stress_hbm, cots_hbm, force_hbm, thick_hbm, switch_hbm)
    targets = (covered_ref, reinit_ref, velo_ref, cotu_ref, stress_ref, cots_ref, force_ref, thick_ref, switch_ref)
    copies = [pltpu.make_async_copy(a, b, sems.at[i]) for i, (a, b) in enumerate(zip(sources, targets))]
    for copy in copies:
        copy.start()
    copies[0].wait()
    heavy = ranked(covered_ref, index_ref, 0) > 1
    for copy in copies[1:]:
        copy.wait()

    def put(block, k, out_ref):
        coef = jnp.where(switch_ref[block] == 1, PLASTIC, VISCOUS)
        out_ref[6 * k] = velo_ref[block]
        out_ref[6 * k + 1] = cotu_ref[block]
        out_ref[6 * k + 2] = stress_ref[block]
        out_ref[6 * k + 3] = cots_ref[block]
        out_ref[6 * k + 4] = force_ref[block]
        out_ref[6 * k + 5] = thick_ref[block] * coef
        return jnp.full((1, 128), 1 - reinit_ref[block], jnp.int32).astype(F32)

    for k in range(SLOTS - 1):
        block = index_ref[jnp.where(heavy, SLOTS + k, 0)]
        send_ref[6 * SLOTS + k // 8, k % 8 : k % 8 + 1, :] = put(block, k, send_ref)
    for k in range(SLOTS):
        block = index_ref[jnp.where(heavy, k, 0)]
        keep_ref[k // 8, k % 8 : k % 8 + 1, :] = put(block, k, own_ref)


def pack_kernel(covered_ref, own_ref, got_ref, keep_ref, out_ref, kept_ref):
    heavy = is_heavy(covered_ref)
    lane = lax.broadcasted_iota(jnp.int32, (8, 128), 1)
    low = lane < 64
    spot = lane % 64

    for k in range(SLOTS):
        tiles = [own_ref[6 * k + f] for f in range(6)]
        if k < SLOTS - 1:
            tiles = [jnp.where(heavy, tile, got_ref[6 * k + f]) for f, tile in enumerate(tiles)]
        for q in range(PARTS):
            shift = (16 - 32 * q) % 128
            for t in range(3):
                both = jnp.where(
                    low,
                    pltpu.roll(tiles[2 * t], shift, 1) if shift else tiles[2 * t],
                    pltpu.roll(tiles[2 * t + 1], (shift + 64) % 128, 1),
                )
                if q == 0:
                    both = jnp.where(spot >= 16, both, 0.0)
                if q == PARTS - 1:
                    both = jnp.where(spot < 48, both, 0.0)
                out_ref[PARTS * k + q, pl.ds(8 * t, 8), :] = both
    slot = lax.axis_index("ice") // PARTS
    mine = jnp.logical_or(heavy, slot == SLOTS - 1)
    sub = slot % 8
    row = jnp.where(
        mine, keep_ref[slot // 8, pl.ds(sub, 1), :], got_ref[6 * SLOTS + slot // 8, pl.ds(sub, 1), :]
    )
    kept_ref[...] = jnp.broadcast_to(row, (8, 128))


def product(a, b, dims):
    a_high = a.astype(BF16)
    a_low = (a - a_high.astype(F32)).astype(BF16)
    b_high = b.astype(BF16)
    b_low = (b - b_high.astype(F32)).astype(BF16)

    def dot(x, y):
        return lax.dot_general(x, y, (dims, ((), ())), preferred_element_type=F32)

    return dot(a_low, b_high) + dot(a_high, b_low) + dot(a_high, b_high)


def spread(v):
    return pl.ds(v, 8, stride=GROUPS)


def work_kernel(
    in_ref, kernel_ref, kept_ref, out_ref,
    x_ref, y_ref, zf_ref, zb_ref, f_ref, acc_ref, af_ref, saved_ref, coef_ref, col_ref,
):
    part = lax.axis_index("ice") % PARTS
    lane = lax.broadcasted_iota(jnp.int32, (8, 128), 1)
    sub = lax.broadcasted_iota(jnp.int32, (8, 128), 0)
    low = lane < 64
    edge = jnp.logical_and(lane % 64 == 16, part == 0)

    last = in_ref[:, 16:24, :].reshape(ROWS, 128)
    col_ref[...] = product(kernel_ref[...], last, ((1,), (0,)))

    def load(v, t):
        return in_ref[pl.ds(v // 8, 8, stride=8), 8 * t + v % 8, :]

    for v in range(GROUPS):
        zeta = col_ref[spread(v), :]
        zb_ref[v] = jnp.where(low, -STEP, zeta)
        zf_ref[v] = jnp.where(low, pltpu.roll(zeta, 64, 1), -STEP)
        x_ref[v] = load(v, 0)
        y_ref[v] = load(v, 1)
        f_ref[v] = jnp.where(low, STEP * load(v, 2), 0.0)
        af_ref[v] = jnp.zeros((8, 128), F32)
        acc_ref[v] = jnp.zeros((8, 128), F32)

    gamma = jnp.full((8, 128), GAMMA, F32)
    for j in range(2 * HALF):
        coef_ref[j] = gamma
    coef_ref[0] = jnp.where(low, GAMMA, 1.0)
    coef_ref[HALF] = GAMMA * kept_ref[...]

    def subcycle(j, late):
        coef = coef_ref[j]
        above = jnp.where(sub == 0, 0.0, pltpu.roll(x_ref[GROUPS - 1], 1, 0))
        first_p = None
        held = None
        for v in range(GROUPS + 1):
            if v < GROUPS:
                x = x_ref[v]
                left = jnp.where(edge, 0.0, pltpu.roll(x, 1, 1))
                strain = (x + x) - above - left
                y = coef * y_ref[v] + zf_ref[v] * strain
                p = zb_ref[v] * y
                both = jnp.where(low, strain, y)
                if late:
                    acc_ref[v] += both * saved_ref[2 * HALF - 1 - j, v]
                else:
                    saved_ref[j, v] = pltpu.roll(both, 64, 1)
                y_ref[v] = y
                af_ref[v] += x
                above = x
                if v == 0:
                    first_p = p
                below = p
            else:
                below = jnp.where(sub == 7, 0.0, pltpu.roll(first_p, 7, 0))
            if v > 0:
                old_x, old_p = held
                right = pltpu.roll(old_p, 127, 1)
                x_ref[v - 1] = BETA * old_x + ((old_p + old_p) - below - right) + f_ref[v - 1]
            held = (x, p)

    for j in range(2 * HALF):
        subcycle(j, j >= HALF)

    for v in range(GROUPS):
        total = acc_ref[v]
        col_ref[spread(v), :] = total + pltpu.roll(total, 64, 1)
    adj_q = product(kernel_ref[...], col_ref[...], ((0,), (0,)))
    for v in range(GROUPS):
        tile = jnp.where(
            lane < 32,
            pltpu.roll(x_ref[v], 48, 1),
            jnp.where(lane < 64, GAMMA * pltpu.roll(y_ref[v], 80, 1), STEP * pltpu.roll(af_ref[v], 16, 1)),
        )
        col_ref[spread(v), :] = tile
    here = jnp.logical_and(lane >= 64, lane < 96)[None]
    moved = pltpu.roll(adj_q, 48, 1).reshape(GROUPS, 8, 128)
    result = jnp.where(here, moved, col_ref[...].reshape(GROUPS, 8, 128))
    out_ref[0] = result
    out_ref[1] = result


def unpack_kernel(covered_ref, back_ref, switch_ref, gu_hbm, gs_hbm, gq_hbm, gf_hbm, all_ref, index_ref, sems):
    heavy = ranked(covered_ref, index_ref, BLOCKS) > 1
    me = lax.axis_index("ocean")
    all_ref[...] = jnp.zeros(all_ref.shape, F32)
    lane = lax.broadcasted_iota(jnp.int32, (8, 128), 1)
    for r in range(MOST):
        block = index_ref[r]
        if r >= SLOTS:
            base = (1 - me) * ICE + PARTS * (r - SLOTS)
        else:
            base = me * ICE + jnp.where(heavy, PARTS * r, PARTS * (SLOTS - 1))
        tiles = [back_ref[base + q] for q in range(PARTS)]
        for f in range(4):
            whole = None
            for q in range(PARTS):
                shift = (32 * (q - f)) % 128
                moved = pltpu.roll(tiles[q], shift, 1) if shift else tiles[q]
                whole = moved if q == 0 else jnp.where(lane >= 32 * q, moved, whole)
            if f == 2:
                inside = jnp.minimum(block, BLOCKS - 1)
                whole = whole * jnp.where(switch_ref[inside] == 1, PLASTIC, VISCOUS)
            all_ref[f, block] = whole
    copies = []
    for f, ref in enumerate((gu_hbm, gs_hbm, gq_hbm, gf_hbm)):
        for part in range(2):
            rows = pl.ds(part * (BLOCKS // 2), BLOCKS // 2)
            copies.append(pltpu.make_async_copy(all_ref.at[f, rows], ref.at[rows], sems.at[2 * f + part]))
    for copy in copies:
        copy.start()
    for copy in copies:
        copy.wait()


def shards(velocity, stress, thickness, forcing, switch, covered, reinit, cot_velocity, cot_stress, kernel):
    tile = (8, 128)

    def sds(*lead):
        return jax.ShapeDtypeStruct(lead + tile, F32)

    params = pltpu.CompilerParams(vmem_limit_bytes=48 * 1024 * 1024)
    own, send, keep = pl.pallas_call(
        gather_kernel,
        name="gather",
        out_shape=(sds(6 * SLOTS), sds(6 * SLOTS + 2), sds(2)),
        in_specs=[pl.BlockSpec(memory_space=pltpu.HBM)] * 9,
        out_specs=(vmem(), vmem(), vmem()),
        scratch_shapes=[pltpu.SMEM((BLOCKS,), jnp.int32)] * 2
        + [pltpu.VMEM((BLOCKS,) + tile, F32)] * 6
        + [pltpu.VMEM((BLOCKS,) + tile, jnp.int32), pltpu.SMEM((MOST + 1,), jnp.int32), pltpu.SemaphoreType.DMA((9,))],
        compiler_params=params,
    )(*[
        pltpu.with_memory_space_constraint(x, pltpu.HBM)
        for x in (covered, reinit, velocity, cot_velocity, stress, cot_stress, forcing, thickness, switch)
    ])
    got = lax.ppermute(send, "ocean", [(0, 1), (1, 0)])
    packed, kept = pl.pallas_call(
        pack_kernel,
        name="pack",
        out_shape=(jax.ShapeDtypeStruct((ICE, 24, 128), F32), sds()),
        in_specs=[smem()] + [vmem()] * 3,
        out_specs=(vmem(), vmem()),
        compiler_params=params,
    )(covered, own, got, keep)
    arrived = lax.all_to_all(packed, "ice", split_axis=0, concat_axis=0, tiled=True)
    col = pltpu.VMEM((GROUPS,) + tile, F32)
    result = pl.pallas_call(
        work_kernel,
        name="work",
        out_shape=sds(2, ICE),
        in_specs=[vmem()] * 3,
        out_specs=vmem(),
        scratch_shapes=[col] * 7
        + [
            pltpu.VMEM((HALF, GROUPS) + tile, F32),
            pltpu.VMEM((2 * HALF,) + tile, F32),
            pltpu.VMEM((ROWS, 128), F32),
        ],
        compiler_params=params,
    )(arrived, kernel, kept)
    back = lax.all_to_all(result.reshape(2 * ICE, 8, 128), ("ocean", "ice"), split_axis=0, concat_axis=0, tiled=True)
    return pl.pallas_call(
        unpack_kernel,
        name="unpack",
        out_shape=(sds(BLOCKS),) * 4,
        in_specs=[smem(), vmem(), vmem()],
        out_specs=(pl.BlockSpec(memory_space=pltpu.HBM),) * 4,
        scratch_shapes=[
            pltpu.VMEM((4, BLOCKS + 1) + tile, F32),
            pltpu.SMEM((MOST + 1,), jnp.int32),
            pltpu.SemaphoreType.DMA((8,)),
        ],
        compiler_params=params,
    )(covered, back, switch)


def solution(mesh):
    cells = P("ocean", "ice", None)
    return jax.shard_map(
        shards,
        mesh=mesh,
        in_specs=(cells, cells, cells, cells, cells, P("ocean"), P("ocean"), cells, cells, P()),
        out_specs=(cells, cells, cells, cells),
        check_vma=False,
    )
```

```python
import jax
import jax.numpy as jnp
from jax import lax
from jax.experimental import pallas as pl
from jax.experimental.pallas import tpu as pltpu
from jax.sharding import PartitionSpec as P

PLASTIC = 0.25
VISCOUS = 1.0
GAMMA = 0.6
BETA = 0.9
STEP = 0.04

HALF = 8
BLOCKS = 64
ICE = 64
SLOTS = 16
PARTS = 4
GROUPS = 64
ROWS = 512
MOST = 31
F32 = jnp.float32
BF16 = jnp.bfloat16


def vmem():
    return pl.BlockSpec(memory_space=pltpu.VMEM)


def smem():
    return pl.BlockSpec(memory_space=pltpu.SMEM)


def ranked(covered_ref, index_ref, empty):
    for k in range(MOST + 1):
        index_ref[k] = empty
    count = jnp.int32(0)
    for b in range(BLOCKS):
        flag = covered_ref[b]
        index_ref[jnp.where(flag == 1, count, MOST)] = b
        count = count + flag
    return count


def gather_kernel(
    covered_hbm, reinit_hbm, velo_hbm, cotu_hbm, stress_hbm, cots_hbm, force_hbm, thick_hbm, switch_hbm,
    own_ref, send_ref, keep_ref,
    covered_ref, reinit_ref, velo_ref, cotu_ref, stress_ref, cots_ref, force_ref, thick_ref, switch_ref,
    index_ref, sems,
):
    sources = (covered_hbm, reinit_hbm, velo_hbm, cotu_hbm, stress_hbm, cots_hbm, force_hbm, thick_hbm, switch_hbm)
    targets = (covered_ref, reinit_ref, velo_ref, cotu_ref, stress_ref, cots_ref, force_ref, thick_ref, switch_ref)
    copies = [pltpu.make_async_copy(a, b, sems.at[i]) for i, (a, b) in enumerate(zip(sources, targets))]
    for copy in copies:
        copy.start()
    copies[0].wait()
    heavy = ranked(covered_ref, index_ref, 0) > 1
    sent = [index_ref[jnp.where(heavy, SLOTS + k, 0)] for k in range(SLOTS - 1)]
    owned = [index_ref[jnp.where(heavy, k, 0)] for k in range(SLOTS)]
    places = [(send_ref, k, block) for k, block in enumerate(sent)] + [(own_ref, k, block) for k, block in enumerate(owned)]
    keep_ref[2] = jnp.full((8, 128), heavy.astype(jnp.int32), jnp.int32).astype(F32)
    copies[1].wait()
    for out_ref, k, block in places:
        row = jnp.full((1, 128), 1 - reinit_ref[block], jnp.int32).astype(F32)
        if out_ref is send_ref:
            send_ref[6 * SLOTS + k // 8, k % 8 : k % 8 + 1, :] = row
        else:
            keep_ref[k // 8, k % 8 : k % 8 + 1, :] = row
    for f in range(5):
        copies[2 + f].wait()
        for out_ref, k, block in places:
            out_ref[6 * k + f] = targets[2 + f][block]
    copies[7].wait()
    copies[8].wait()
    for out_ref, k, block in places:
        coef = jnp.where(switch_ref[block] == 1, PLASTIC, VISCOUS)
        out_ref[6 * k + 5] = thick_ref[block] * coef


def split(x):
    high = x.astype(BF16)
    return high, (x - high.astype(F32)).astype(BF16)


def split_kernel(kernel_ref, halves_ref):
    whole = kernel_ref[...]
    halves_ref[0], halves_ref[1] = split(whole)
    halves_ref[2], halves_ref[3] = split(whole.T)


def pack_kernel(own_ref, got_ref, keep_ref, out_ref, kept_ref):
    heavy = keep_ref[2] > 0.5
    lane = lax.broadcasted_iota(jnp.int32, (8, 128), 1)
    low = lane < 64
    spot = lane % 64

    for k in range(SLOTS):
        tiles = [own_ref[6 * k + f] for f in range(6)]
        if k < SLOTS - 1:
            tiles = [jnp.where(heavy, tile, got_ref[6 * k + f]) for f, tile in enumerate(tiles)]
        for q in range(PARTS):
            shift = (16 - 32 * q) % 128
            for t in range(3):
                both = jnp.where(
                    low,
                    pltpu.roll(tiles[2 * t], shift, 1) if shift else tiles[2 * t],
                    pltpu.roll(tiles[2 * t + 1], (shift + 64) % 128, 1),
                )
                if q == 0:
                    both = jnp.where(spot >= 16, both, 0.0)
                if q == PARTS - 1:
                    both = jnp.where(spot < 48, both, 0.0)
                out_ref[PARTS * k + q, pl.ds(8 * t, 8), :] = both
    slot = lax.axis_index("ice") // PARTS
    sub = slot % 8
    mine = jnp.broadcast_to(keep_ref[slot // 8, pl.ds(sub, 1), :], (8, 128))
    other = jnp.broadcast_to(got_ref[6 * SLOTS + slot // 8, pl.ds(sub, 1), :], (8, 128))
    own_slot = jnp.full((8, 128), slot, jnp.int32) == SLOTS - 1
    kept_ref[...] = jnp.where(jnp.logical_or(heavy, own_slot), mine, other)


def product(a_high, a_low, b):
    b_high, b_low = split(b)

    def dot(x, y):
        return jnp.dot(x, y, preferred_element_type=F32)

    wide = dot(a_high, jnp.concatenate([b_high, b_low], axis=1))
    return (dot(a_low, b_high) + wide[:, 128:]) + wide[:, :128]


def spread(v):
    return pl.ds(v, 8, stride=GROUPS)


def work_kernel(
    in_ref, halves_ref, kept_ref, out_ref,
    x_ref, y_ref, zf_ref, zb_ref, f_ref, acc_ref, af_ref, saved_ref, coef_ref, col_ref,
):
    part = lax.axis_index("ice") % PARTS
    lane = lax.broadcasted_iota(jnp.int32, (8, 128), 1)
    sub = lax.broadcasted_iota(jnp.int32, (8, 128), 0)
    low = lane < 64
    edge = jnp.logical_and(lane % 64 == 16, part == 0)

    last = in_ref[:, 16:24, :].reshape(ROWS, 128)
    col_ref[...] = product(halves_ref[0], halves_ref[1], last)

    def load(v, t):
        return in_ref[pl.ds(v // 8, 8, stride=8), 8 * t + v % 8, :]

    for v in range(GROUPS):
        zeta = col_ref[spread(v), :]
        zb_ref[v] = jnp.where(low, -STEP, zeta)
        zf_ref[v] = jnp.where(low, pltpu.roll(zeta, 64, 1), -STEP)
        x_ref[v] = load(v, 0)
        y_ref[v] = load(v, 1)
        f_ref[v] = jnp.where(low, STEP * load(v, 2), 0.0)
        af_ref[v] = jnp.zeros((8, 128), F32)
        acc_ref[v] = jnp.zeros((8, 128), F32)

    gamma = jnp.full((8, 128), GAMMA, F32)
    for j in range(2 * HALF):
        coef_ref[j] = gamma
    coef_ref[0] = jnp.where(low, GAMMA, 1.0)
    coef_ref[HALF] = GAMMA * kept_ref[...]

    def subcycle(j, late):
        coef = coef_ref[j]
        above = jnp.where(sub == 0, 0.0, pltpu.roll(x_ref[GROUPS - 1], 1, 0))
        first_p = None
        held = None
        for v in range(GROUPS + 1):
            if v < GROUPS:
                x = x_ref[v]
                left = jnp.where(edge, 0.0, pltpu.roll(x, 1, 1))
                strain = (x + x) - above - left
                y = coef * y_ref[v] + zf_ref[v] * strain
                p = zb_ref[v] * y
                both = jnp.where(low, strain, y)
                if late:
                    acc_ref[v] += both * saved_ref[2 * HALF - 1 - j, v]
                else:
                    saved_ref[j, v] = pltpu.roll(both, 64, 1)
                y_ref[v] = y
                af_ref[v] += x
                above = x
                if v == 0:
                    first_p = p
                below = p
            else:
                below = jnp.where(sub == 7, 0.0, pltpu.roll(first_p, 7, 0))
            if v > 0:
                old_x, old_p = held
                right = pltpu.roll(old_p, 127, 1)
                x_ref[v - 1] = BETA * old_x + ((old_p + old_p) - below - right) + f_ref[v - 1]
            held = (x, p)

    for j in range(2 * HALF):
        subcycle(j, j >= HALF)

    for v in range(GROUPS):
        total = acc_ref[v]
        col_ref[spread(v), :] = total + pltpu.roll(total, 64, 1)
    adj_q = product(halves_ref[2], halves_ref[3], col_ref[...])
    for v in range(GROUPS):
        tile = jnp.where(
            lane < 32,
            pltpu.roll(x_ref[v], 48, 1),
            jnp.where(lane < 64, GAMMA * pltpu.roll(y_ref[v], 80, 1), STEP * pltpu.roll(af_ref[v], 16, 1)),
        )
        col_ref[spread(v), :] = tile
    here = jnp.logical_and(lane >= 64, lane < 96)[None]
    moved = pltpu.roll(adj_q, 48, 1).reshape(GROUPS, 8, 128)
    result = jnp.where(here, moved, col_ref[...].reshape(GROUPS, 8, 128))
    out_ref[0] = result
    out_ref[1] = result


def unpack_kernel(covered_ref, back_ref, switch_ref, gu_hbm, gs_hbm, gq_hbm, gf_hbm, all_ref, index_ref, sems):
    heavy = ranked(covered_ref, index_ref, BLOCKS) > 1
    me = lax.axis_index("ocean")
    lane = lax.broadcasted_iota(jnp.int32, (8, 128), 1)
    blocks = [index_ref[r] for r in range(MOST)]
    copies = []
    for f, ref in enumerate((gu_hbm, gs_hbm, gf_hbm, gq_hbm)):
        f = (0, 1, 3, 2)[f]
        all_ref[f] = jnp.zeros(all_ref.shape[1:], F32)
        for r, block in enumerate(blocks):
            if r >= SLOTS:
                base = (1 - me) * ICE + PARTS * (r - SLOTS)
            else:
                base = me * ICE + jnp.where(heavy, PARTS * r, PARTS * (SLOTS - 1))
            whole = None
            for q in range(PARTS):
                shift = (32 * (q - f)) % 128
                moved = back_ref[base + q]
                if shift:
                    moved = pltpu.roll(moved, shift, 1)
                whole = moved if q == 0 else jnp.where(lane >= 32 * q, moved, whole)
            if f == 2:
                inside = jnp.minimum(block, BLOCKS - 1)
                whole = whole * jnp.where(switch_ref[inside] == 1, PLASTIC, VISCOUS)
            all_ref[f, block] = whole
        copy = pltpu.make_async_copy(all_ref.at[f, pl.ds(0, BLOCKS)], ref, sems.at[f])
        copy.start()
        copies.append(copy)
    for copy in copies:
        copy.wait()


def shards(velocity, stress, thickness, forcing, switch, covered, reinit, cot_velocity, cot_stress, kernel):
    tile = (8, 128)

    def sds(*lead):
        return jax.ShapeDtypeStruct(lead + tile, F32)

    params = pltpu.CompilerParams(vmem_limit_bytes=12 * 1024 * 1024)
    own, send, keep = pl.pallas_call(
        gather_kernel,
        name="gather",
        out_shape=(sds(6 * SLOTS), sds(6 * SLOTS + 2), sds(3)),
        in_specs=[pl.BlockSpec(memory_space=pltpu.HBM)] * 9,
        out_specs=(vmem(), vmem(), vmem()),
        scratch_shapes=[pltpu.SMEM((BLOCKS,), jnp.int32)] * 2
        + [pltpu.VMEM((BLOCKS,) + tile, F32)] * 6
        + [pltpu.VMEM((BLOCKS,) + tile, jnp.int32), pltpu.SMEM((MOST + 1,), jnp.int32), pltpu.SemaphoreType.DMA((9,))],
        compiler_params=params,
    )(*[
        pltpu.with_memory_space_constraint(x, pltpu.HBM)
        for x in (covered, reinit, velocity, cot_velocity, stress, cot_stress, forcing, thickness, switch)
    ])
    got = lax.ppermute(send, "ocean", [(0, 1), (1, 0)])
    halves = pl.pallas_call(
        split_kernel,
        name="split",
        out_shape=jax.ShapeDtypeStruct((4, ROWS, ROWS), BF16),
        in_specs=[vmem()],
        out_specs=vmem(),
        compiler_params=params,
    )(kernel)
    packed, kept = pl.pallas_call(
        pack_kernel,
        name="pack",
        out_shape=(jax.ShapeDtypeStruct((ICE, 24, 128), F32), sds()),
        in_specs=[vmem()] * 3,
        out_specs=(vmem(), vmem()),
        compiler_params=params,
    )(own, got, keep)
    arrived = lax.all_to_all(packed, "ice", split_axis=0, concat_axis=0, tiled=True)
    col = pltpu.VMEM((GROUPS,) + tile, F32)
    result = pl.pallas_call(
        work_kernel,
        name="work",
        out_shape=sds(2, ICE),
        in_specs=[vmem()] * 3,
        out_specs=vmem(),
        scratch_shapes=[col] * 7
        + [
            pltpu.VMEM((HALF, GROUPS) + tile, F32),
            pltpu.VMEM((2 * HALF,) + tile, F32),
            pltpu.VMEM((ROWS, 128), F32),
        ],
        compiler_params=params,
    )(arrived, halves, kept)
    back = lax.all_to_all(result.reshape(2 * ICE, 8, 128), ("ocean", "ice"), split_axis=0, concat_axis=0, tiled=True)
    return pl.pallas_call(
        unpack_kernel,
        name="unpack",
        out_shape=(sds(BLOCKS),) * 4,
        in_specs=[smem(), vmem(), vmem()],
        out_specs=(pl.BlockSpec(memory_space=pltpu.HBM),) * 4,
        scratch_shapes=[
            pltpu.VMEM((4, BLOCKS + 1) + tile, F32),
            pltpu.SMEM((MOST + 1,), jnp.int32),
            pltpu.SemaphoreType.DMA((4,)),
        ],
        compiler_params=params,
    )(covered, back, switch)


def solution(mesh):
    cells = P("ocean", "ice", None)
    return jax.shard_map(
        shards,
        mesh=mesh,
        in_specs=(cells, cells, cells, cells, cells, P("ocean"), P("ocean"), cells, cells, P()),
        out_specs=(cells, cells, cells, cells),
        check_vma=False,
    )
```

```python
import jax
import jax.numpy as jnp
from jax import lax
from jax.experimental import pallas as pl
from jax.experimental.pallas import tpu as pltpu
from jax.sharding import PartitionSpec as P

PLASTIC = 0.25
VISCOUS = 1.0
GAMMA = 0.6
BETA = 0.9
STEP = 0.04

HALF = 8
BLOCKS = 64
ICE = 64
SLOTS = 16
PARTS = 4
GROUPS = 64
ROWS = 512
MOST = 31
F32 = jnp.float32
BF16 = jnp.bfloat16


def vmem():
    return pl.BlockSpec(memory_space=pltpu.VMEM)


def smem():
    return pl.BlockSpec(memory_space=pltpu.SMEM)


def ranked(covered_ref, index_ref, empty):
    for k in range(MOST + 1):
        index_ref[k] = empty
    count = jnp.int32(0)
    for b in range(BLOCKS):
        flag = covered_ref[b]
        index_ref[jnp.where(flag == 1, count, MOST)] = b
        count = count + flag
    return count


def gather_kernel(
    covered_hbm, reinit_hbm, velo_hbm, cotu_hbm, stress_hbm, cots_hbm, force_hbm, thick_hbm, switch_hbm,
    own_ref, send_ref, keep_ref,
    covered_ref, reinit_ref, velo_ref, cotu_ref, stress_ref, cots_ref, force_ref, thick_ref, switch_ref,
    index_ref, sems,
):
    sources = (covered_hbm, reinit_hbm, velo_hbm, cotu_hbm, stress_hbm, cots_hbm, force_hbm, thick_hbm, switch_hbm)
    targets = (covered_ref, reinit_ref, velo_ref, cotu_ref, stress_ref, cots_ref, force_ref, thick_ref, switch_ref)
    copies = [pltpu.make_async_copy(a, b, sems.at[i]) for i, (a, b) in enumerate(zip(sources, targets))]
    for copy in copies:
        copy.start()
    copies[0].wait()
    heavy = ranked(covered_ref, index_ref, 0) > 1
    sent = [index_ref[jnp.where(heavy, SLOTS + k, 0)] for k in range(SLOTS - 1)]
    owned = [index_ref[jnp.where(heavy, k, 0)] for k in range(SLOTS)]
    places = [(send_ref, k, block) for k, block in enumerate(sent)] + [(own_ref, k, block) for k, block in enumerate(owned)]
    keep_ref[2] = jnp.full((8, 128), heavy.astype(jnp.int32), jnp.int32).astype(F32)
    copies[1].wait()
    for out_ref, k, block in places:
        row = jnp.full((1, 128), 1 - reinit_ref[block], jnp.int32).astype(F32)
        if out_ref is send_ref:
            send_ref[6 * SLOTS + k // 8, k % 8 : k % 8 + 1, :] = row
        else:
            keep_ref[k // 8, k % 8 : k % 8 + 1, :] = row
    for f in range(5):
        copies[2 + f].wait()
        for out_ref, k, block in places:
            out_ref[6 * k + f] = targets[2 + f][block]
    copies[7].wait()
    copies[8].wait()
    for out_ref, k, block in places:
        coef = jnp.where(switch_ref[block] == 1, PLASTIC, VISCOUS)
        out_ref[6 * k + 5] = thick_ref[block] * coef


def split(x):
    high = x.astype(BF16)
    return high, (x - high.astype(F32)).astype(BF16)


def split_kernel(kernel_ref, halves_ref):
    whole = kernel_ref[...]
    halves_ref[0], halves_ref[1] = split(whole)
    halves_ref[2], halves_ref[3] = split(whole.T)


def pack_kernel(own_ref, got_ref, keep_ref, out_ref, kept_ref):
    heavy = keep_ref[2] > 0.5
    lane = lax.broadcasted_iota(jnp.int32, (8, 128), 1)
    low = lane < 64
    spot = lane % 64

    for k in range(SLOTS):
        tiles = [own_ref[6 * k + f] for f in range(6)]
        if k < SLOTS - 1:
            tiles = [jnp.where(heavy, tile, got_ref[6 * k + f]) for f, tile in enumerate(tiles)]
        for q in range(PARTS):
            shift = (16 - 32 * q) % 128
            for t in range(3):
                both = jnp.where(
                    low,
                    pltpu.roll(tiles[2 * t], shift, 1) if shift else tiles[2 * t],
                    pltpu.roll(tiles[2 * t + 1], (shift + 64) % 128, 1),
                )
                if q == 0:
                    both = jnp.where(spot >= 16, both, 0.0)
                if q == PARTS - 1:
                    both = jnp.where(spot < 48, both, 0.0)
                out_ref[PARTS * k + q, pl.ds(8 * t, 8), :] = both
    slot = lax.axis_index("ice") // PARTS
    sub = slot % 8
    mine = jnp.broadcast_to(keep_ref[slot // 8, pl.ds(sub, 1), :], (8, 128))
    other = jnp.broadcast_to(got_ref[6 * SLOTS + slot // 8, pl.ds(sub, 1), :], (8, 128))
    own_slot = jnp.full((8, 128), slot, jnp.int32) == SLOTS - 1
    kept_ref[...] = jnp.where(jnp.logical_or(heavy, own_slot), mine, other)


def product(a_high, a_low, b):
    b_high, b_low = split(b)

    def dot(x, y):
        return jnp.dot(x, y, preferred_element_type=F32)

    wide = dot(a_high, jnp.concatenate([b_high, b_low], axis=1))
    return (dot(a_low, b_high) + wide[:, 128:]) + wide[:, :128]


def spread(v):
    return pl.ds(v, 8, stride=GROUPS)


def work_kernel(
    in_ref, halves_ref, kept_ref, out_ref,
    x_ref, y_ref, zf_ref, zb_ref, f_ref, acc_ref, af_ref, saved_ref, coef_ref, col_ref,
):
    part = lax.axis_index("ice") % PARTS
    lane = lax.broadcasted_iota(jnp.int32, (8, 128), 1)
    sub = lax.broadcasted_iota(jnp.int32, (8, 128), 0)
    low = lane < 64
    edge = jnp.logical_and(lane % 64 == 16, part == 0)

    last = in_ref[:, 16:24, :].reshape(ROWS, 128)
    col_ref[...] = product(halves_ref[0], halves_ref[1], last)

    def load(v, t):
        return in_ref[pl.ds(v // 8, 8, stride=8), 8 * t + v % 8, :]

    for v in range(GROUPS):
        zeta = col_ref[spread(v), :]
        zb_ref[v] = jnp.where(low, -STEP, zeta)
        zf_ref[v] = jnp.where(low, pltpu.roll(zeta, 64, 1), -STEP)
        x_ref[v] = load(v, 0)
        y_ref[v] = load(v, 1)
        f_ref[v] = jnp.where(low, STEP * load(v, 2), 0.0)
        af_ref[v] = jnp.zeros((8, 128), F32)
        acc_ref[v] = jnp.zeros((8, 128), F32)

    gamma = jnp.full((8, 128), GAMMA, F32)
    for j in range(2 * HALF):
        coef_ref[j] = gamma
    coef_ref[0] = jnp.where(low, GAMMA, 1.0)
    coef_ref[HALF] = GAMMA * kept_ref[...]

    def subcycle(j, late):
        coef = coef_ref[j]
        above = jnp.where(sub == 0, 0.0, pltpu.roll(x_ref[GROUPS - 1], 1, 0))
        first_p = None
        held = None
        for v in range(GROUPS + 1):
            if v < GROUPS:
                x = x_ref[v]
                left = jnp.where(edge, 0.0, pltpu.roll(x, 1, 1))
                strain = 2.0 * x - (above + left)
                y = coef * y_ref[v] + zf_ref[v] * strain
                p = zb_ref[v] * y
                both = jnp.where(low, strain, y)
                if late:
                    acc_ref[v] += both * pltpu.roll(saved_ref[2 * HALF - 1 - j, v], 64, 1)
                else:
                    saved_ref[j, v] = both
                y_ref[v] = y
                af_ref[v] += x
                above = x
                if v == 0:
                    first_p = p
                below = p
            else:
                below = jnp.where(sub == 7, 0.0, pltpu.roll(first_p, 7, 0))
            if v > 0:
                old_x, old_p = held
                right = pltpu.roll(old_p, 127, 1)
                x_ref[v - 1] = BETA * old_x + (2.0 * old_p - (below + right)) + f_ref[v - 1]
            held = (x, p)

    for j in range(2 * HALF):
        subcycle(j, j >= HALF)

    for v in range(GROUPS):
        total = acc_ref[v]
        col_ref[spread(v), :] = total + pltpu.roll(total, 64, 1)
    adj_q = product(halves_ref[2], halves_ref[3], col_ref[...])
    for v in range(GROUPS):
        tile = jnp.where(
            lane < 32,
            pltpu.roll(x_ref[v], 48, 1),
            jnp.where(lane < 64, GAMMA * pltpu.roll(y_ref[v], 80, 1), STEP * pltpu.roll(af_ref[v], 16, 1)),
        )
        col_ref[spread(v), :] = tile
    here = jnp.logical_and(lane >= 64, lane < 96)[None]
    moved = pltpu.roll(adj_q, 48, 1).reshape(GROUPS, 8, 128)
    result = jnp.where(here, moved, col_ref[...].reshape(GROUPS, 8, 128))
    out_ref[0] = result
    out_ref[1] = result


def unpack_kernel(covered_ref, back_ref, switch_ref, gu_hbm, gs_hbm, gq_hbm, gf_hbm, all_ref, index_ref, sems):
    heavy = ranked(covered_ref, index_ref, BLOCKS) > 1
    me = lax.axis_index("ocean")
    lane = lax.broadcasted_iota(jnp.int32, (8, 128), 1)
    blocks = [index_ref[r] for r in range(MOST)]
    copies = []
    for f, ref in enumerate((gu_hbm, gs_hbm, gf_hbm, gq_hbm)):
        f = (0, 1, 3, 2)[f]
        all_ref[f] = jnp.zeros(all_ref.shape[1:], F32)
        for r, block in enumerate(blocks):
            if r >= SLOTS:
                base = (1 - me) * ICE + PARTS * (r - SLOTS)
            else:
                base = me * ICE + jnp.where(heavy, PARTS * r, PARTS * (SLOTS - 1))
            whole = None
            for q in range(PARTS):
                shift = (32 * (q - f)) % 128
                moved = back_ref[base + q]
                if shift:
                    moved = pltpu.roll(moved, shift, 1)
                whole = moved if q == 0 else jnp.where(lane >= 32 * q, moved, whole)
            if f == 2:
                inside = jnp.minimum(block, BLOCKS - 1)
                whole = whole * jnp.where(switch_ref[inside] == 1, PLASTIC, VISCOUS)
            all_ref[f, block] = whole
        copy = pltpu.make_async_copy(all_ref.at[f, pl.ds(0, BLOCKS)], ref, sems.at[f])
        copy.start()
        copies.append(copy)
    for copy in copies:
        copy.wait()


def shards(velocity, stress, thickness, forcing, switch, covered, reinit, cot_velocity, cot_stress, kernel):
    tile = (8, 128)

    def sds(*lead):
        return jax.ShapeDtypeStruct(lead + tile, F32)

    params = pltpu.CompilerParams(vmem_limit_bytes=12 * 1024 * 1024)
    own, send, keep = pl.pallas_call(
        gather_kernel,
        name="gather",
        out_shape=(sds(6 * SLOTS), sds(6 * SLOTS + 2), sds(3)),
        in_specs=[pl.BlockSpec(memory_space=pltpu.HBM)] * 9,
        out_specs=(vmem(), vmem(), vmem()),
        scratch_shapes=[pltpu.SMEM((BLOCKS,), jnp.int32)] * 2
        + [pltpu.VMEM((BLOCKS,) + tile, F32)] * 6
        + [pltpu.VMEM((BLOCKS,) + tile, jnp.int32), pltpu.SMEM((MOST + 1,), jnp.int32), pltpu.SemaphoreType.DMA((9,))],
        compiler_params=params,
    )(*[
        pltpu.with_memory_space_constraint(x, pltpu.HBM)
        for x in (covered, reinit, velocity, cot_velocity, stress, cot_stress, forcing, thickness, switch)
    ])
    got = lax.ppermute(send, "ocean", [(0, 1), (1, 0)])
    halves = pl.pallas_call(
        split_kernel,
        name="split",
        out_shape=jax.ShapeDtypeStruct((4, ROWS, ROWS), BF16),
        in_specs=[vmem()],
        out_specs=vmem(),
        compiler_params=params,
    )(kernel)
    packed, kept = pl.pallas_call(
        pack_kernel,
        name="pack",
        out_shape=(jax.ShapeDtypeStruct((ICE, 24, 128), F32), sds()),
        in_specs=[vmem()] * 3,
        out_specs=(vmem(), vmem()),
        compiler_params=params,
    )(own, got, keep)
    arrived = lax.all_to_all(packed, "ice", split_axis=0, concat_axis=0, tiled=True)
    col = pltpu.VMEM((GROUPS,) + tile, F32)
    result = pl.pallas_call(
        work_kernel,
        name="work",
        out_shape=sds(2, ICE),
        in_specs=[vmem()] * 3,
        out_specs=vmem(),
        scratch_shapes=[col] * 7
        + [
            pltpu.VMEM((HALF, GROUPS) + tile, F32),
            pltpu.VMEM((2 * HALF,) + tile, F32),
            pltpu.VMEM((ROWS, 128), F32),
        ],
        compiler_params=params,
    )(arrived, halves, kept)
    back = lax.all_to_all(result.reshape(2 * ICE, 8, 128), ("ocean", "ice"), split_axis=0, concat_axis=0, tiled=True)
    return pl.pallas_call(
        unpack_kernel,
        name="unpack",
        out_shape=(sds(BLOCKS),) * 4,
        in_specs=[smem(), vmem(), vmem()],
        out_specs=(pl.BlockSpec(memory_space=pltpu.HBM),) * 4,
        scratch_shapes=[
            pltpu.VMEM((4, BLOCKS + 1) + tile, F32),
            pltpu.SMEM((MOST + 1,), jnp.int32),
            pltpu.SemaphoreType.DMA((4,)),
        ],
        compiler_params=params,
    )(covered, back, switch)


def solution(mesh):
    cells = P("ocean", "ice", None)
    return jax.shard_map(
        shards,
        mesh=mesh,
        in_specs=(cells, cells, cells, cells, cells, P("ocean"), P("ocean"), cells, cells, P()),
        out_specs=(cells, cells, cells, cells),
        check_vma=False,
    )
```

```python
import jax
import jax.numpy as jnp
from jax import lax
from jax.experimental import pallas as pl
from jax.experimental.pallas import tpu as pltpu
from jax.sharding import PartitionSpec as P

PLASTIC = 0.25
VISCOUS = 1.0
GAMMA = 0.6
BETA = 0.9
STEP = 0.04

HALF = 8
BLOCKS = 64
ICE = 64
SLOTS = 16
PARTS = 4
GROUPS = 64
ROWS = 512
MOST = 31
F32 = jnp.float32
BF16 = jnp.bfloat16


def vmem():
    return pl.BlockSpec(memory_space=pltpu.VMEM)


def smem():
    return pl.BlockSpec(memory_space=pltpu.SMEM)


def ranked(covered_ref, index_ref, empty):
    for k in range(MOST + 1):
        index_ref[k] = empty
    count = jnp.int32(0)
    for b in range(BLOCKS):
        flag = covered_ref[b]
        index_ref[jnp.where(flag == 1, count, MOST)] = b
        count = count + flag
    return count


def gather_kernel(
    covered_hbm, reinit_hbm, velo_hbm, cotu_hbm, stress_hbm, cots_hbm, force_hbm, thick_hbm, switch_hbm,
    own_ref, send_ref, keep_ref,
    covered_ref, reinit_ref, velo_ref, cotu_ref, stress_ref, cots_ref, force_ref, thick_ref, switch_ref,
    index_ref, sems,
):
    sources = (covered_hbm, reinit_hbm, velo_hbm, cotu_hbm, stress_hbm, cots_hbm, force_hbm, thick_hbm, switch_hbm)
    targets = (covered_ref, reinit_ref, velo_ref, cotu_ref, stress_ref, cots_ref, force_ref, thick_ref, switch_ref)
    copies = [pltpu.make_async_copy(a, b, sems.at[i]) for i, (a, b) in enumerate(zip(sources, targets))]
    for copy in copies:
        copy.start()
    copies[0].wait()
    heavy = ranked(covered_ref, index_ref, 0) > 1
    sent = [index_ref[jnp.where(heavy, SLOTS + k, 0)] for k in range(SLOTS - 1)]
    owned = [index_ref[jnp.where(heavy, k, 0)] for k in range(SLOTS)]
    places = [(send_ref, k, block) for k, block in enumerate(sent)] + [(own_ref, k, block) for k, block in enumerate(owned)]
    keep_ref[2] = jnp.full((8, 128), heavy.astype(jnp.int32), jnp.int32).astype(F32)
    copies[1].wait()
    for out_ref, k, block in places:
        row = jnp.full((1, 128), 1 - reinit_ref[block], jnp.int32).astype(F32)
        if out_ref is send_ref:
            send_ref[6 * SLOTS + k // 8, k % 8 : k % 8 + 1, :] = row
        else:
            keep_ref[k // 8, k % 8 : k % 8 + 1, :] = row
    for f in range(5):
        copies[2 + f].wait()
        for out_ref, k, block in places:
            out_ref[6 * k + f] = targets[2 + f][block]
    copies[7].wait()
    copies[8].wait()
    for out_ref, k, block in places:
        coef = jnp.where(switch_ref[block] == 1, PLASTIC, VISCOUS)
        out_ref[6 * k + 5] = thick_ref[block] * coef


def split(x):
    high = x.astype(BF16)
    return high, (x - high.astype(F32)).astype(BF16)


def split_kernel(kernel_ref, halves_ref):
    whole = kernel_ref[...]
    halves_ref[0], halves_ref[1] = split(whole)
    halves_ref[2], halves_ref[3] = split(whole.T)


def pack_kernel(own_ref, got_ref, keep_ref, out_ref, kept_ref):
    heavy = keep_ref[2] > 0.5
    lane = lax.broadcasted_iota(jnp.int32, (8, 128), 1)
    low = lane < 64
    spot = lane % 64

    for k in range(SLOTS):
        tiles = [own_ref[6 * k + f] for f in range(6)]
        if k < SLOTS - 1:
            tiles = [jnp.where(heavy, tile, got_ref[6 * k + f]) for f, tile in enumerate(tiles)]
        for q in range(PARTS):
            shift = (16 - 32 * q) % 128
            for t in range(3):
                both = jnp.where(
                    low,
                    pltpu.roll(tiles[2 * t], shift, 1) if shift else tiles[2 * t],
                    pltpu.roll(tiles[2 * t + 1], (shift + 64) % 128, 1),
                )
                if q == 0:
                    both = jnp.where(spot >= 16, both, 0.0)
                if q == PARTS - 1:
                    both = jnp.where(spot < 48, both, 0.0)
                out_ref[PARTS * k + q, pl.ds(8 * t, 8), :] = both
    slot = lax.axis_index("ice") // PARTS
    sub = slot % 8
    mine = jnp.broadcast_to(keep_ref[slot // 8, pl.ds(sub, 1), :], (8, 128))
    other = jnp.broadcast_to(got_ref[6 * SLOTS + slot // 8, pl.ds(sub, 1), :], (8, 128))
    own_slot = jnp.full((8, 128), slot, jnp.int32) == SLOTS - 1
    kept_ref[...] = jnp.where(jnp.logical_or(heavy, own_slot), mine, other)


def product(a_high, a_low, b):
    b_high, b_low = split(b)

    def dot(x, y):
        return jnp.dot(x, y, preferred_element_type=F32)

    wide = dot(a_high, jnp.concatenate([b_high, b_low], axis=1))
    return (dot(a_low, b_high) + wide[:, 128:]) + wide[:, :128]


def spread(v):
    return pl.ds(v, 8, stride=GROUPS)


def work_kernel(
    in_ref, halves_ref, kept_ref, out_ref,
    x_ref, y_ref, zf_ref, zb_ref, f_ref, acc_ref, af_ref, saved_ref, coef_ref, col_ref,
):
    part = lax.axis_index("ice") % PARTS
    lane = lax.broadcasted_iota(jnp.int32, (8, 128), 1)
    sub = lax.broadcasted_iota(jnp.int32, (8, 128), 0)
    low = lane < 64
    edge = jnp.logical_and(lane % 64 == 16, part == 0)

    last = in_ref[:, 16:24, :].reshape(ROWS, 128)
    col_ref[...] = product(halves_ref[0], halves_ref[1], last)

    def load(v, t):
        return in_ref[pl.ds(v // 8, 8, stride=8), 8 * t + v % 8, :]

    for v in range(GROUPS):
        zeta = col_ref[spread(v), :]
        zb_ref[v] = jnp.where(low, -STEP, zeta)
        zf_ref[v] = jnp.where(low, pltpu.roll(zeta, 64, 1), -STEP)
        x_ref[v] = load(v, 0)
        y_ref[v] = load(v, 1)
        f_ref[v] = jnp.where(low, STEP * load(v, 2), 0.0)
        af_ref[v] = jnp.zeros((8, 128), F32)
        acc_ref[v] = jnp.zeros((8, 128), F32)

    gamma = jnp.full((8, 128), GAMMA, F32)
    for j in range(2 * HALF):
        coef_ref[j] = gamma
    coef_ref[0] = jnp.where(low, GAMMA, 1.0)
    coef_ref[HALF] = GAMMA * kept_ref[...]

    def subcycle(j, late):
        coef = coef_ref[j]
        above = jnp.where(sub == 0, 0.0, pltpu.roll(x_ref[GROUPS - 1], 1, 0))
        first_p = None
        held = None
        for v in range(GROUPS + 1):
            if v < GROUPS:
                x = x_ref[v]
                left = jnp.where(edge, 0.0, pltpu.roll(x, 1, 1))
                strain = 2.0 * x - (above + left)
                y = coef * y_ref[v] + zf_ref[v] * strain
                p = zb_ref[v] * y
                both = jnp.where(low, strain, y)
                if late:
                    acc_ref[v] += both * pltpu.roll(saved_ref[2 * HALF - 1 - j, v], 64, 1)
                else:
                    saved_ref[j, v] = both
                y_ref[v] = y
                af_ref[v] += x
                above = x
                if v == 0:
                    first_p = p
                below = p
            else:
                below = jnp.where(sub == 7, 0.0, pltpu.roll(first_p, 7, 0))
            if v > 0:
                old_x, old_p = held
                right = pltpu.roll(old_p, 127, 1)
                x_ref[v - 1] = BETA * old_x + (2.0 * old_p - (below + right)) + f_ref[v - 1]
            held = (x, p)

    for j in range(2 * HALF):
        subcycle(j, j >= HALF)

    for v in range(GROUPS):
        total = acc_ref[v]
        col_ref[spread(v), :] = total + pltpu.roll(total, 64, 1)
    adj_q = product(halves_ref[2], halves_ref[3], col_ref[...])
    for v in range(GROUPS):
        tile = jnp.where(
            lane < 32,
            pltpu.roll(x_ref[v], 48, 1),
            jnp.where(lane < 64, GAMMA * pltpu.roll(y_ref[v], 80, 1), STEP * pltpu.roll(af_ref[v], 16, 1)),
        )
        col_ref[spread(v), :] = tile
    here = jnp.logical_and(lane >= 64, lane < 96)[None]
    moved = pltpu.roll(adj_q, 48, 1).reshape(GROUPS, 8, 128)
    result = jnp.where(here, moved, col_ref[...].reshape(GROUPS, 8, 128))
    out_ref[...] = result


def unpack(back_ref, switch_ref, all_ref, f, base, block):
    lane = lax.broadcasted_iota(jnp.int32, (8, 128), 1)
    whole = None
    for q in range(PARTS):
        shift = (32 * (q - f)) % 128
        moved = back_ref[base + q]
        if shift:
            moved = pltpu.roll(moved, shift, 1)
        whole = moved if q == 0 else jnp.where(lane >= 32 * q, moved, whole)
    if f == 2:
        inside = jnp.minimum(block, BLOCKS - 1)
        whole = whole * jnp.where(switch_ref[inside] == 1, PLASTIC, VISCOUS)
    all_ref[f, block] = whole


def near_kernel(covered_ref, back_ref, switch_ref, all_ref, index_ref):
    heavy = ranked(covered_ref, index_ref, BLOCKS) > 1
    blocks = [index_ref[r] for r in range(SLOTS)]
    for f in range(4):
        all_ref[f] = jnp.zeros(all_ref.shape[1:], F32)
        for r, block in enumerate(blocks):
            base = jnp.where(heavy, PARTS * r, PARTS * (SLOTS - 1))
            unpack(back_ref, switch_ref, all_ref, f, base, block)


def far_kernel(index_ref, far_ref, switch_ref, near_ref, gu_hbm, gs_hbm, gq_hbm, gf_hbm, all_ref, sems):
    copies = []
    for f, ref in ((0, gu_hbm), (1, gs_hbm), (3, gf_hbm), (2, gq_hbm)):
        for r in range(SLOTS, MOST):
            unpack(far_ref, switch_ref, all_ref, f, PARTS * (r - SLOTS), index_ref[r])
        copy = pltpu.make_async_copy(all_ref.at[f, pl.ds(0, BLOCKS)], ref, sems.at[f])
        copy.start()
        copies.append(copy)
    for copy in copies:
        copy.wait()


def shards(velocity, stress, thickness, forcing, switch, covered, reinit, cot_velocity, cot_stress, kernel):
    tile = (8, 128)

    def sds(*lead):
        return jax.ShapeDtypeStruct(lead + tile, F32)

    params = pltpu.CompilerParams(vmem_limit_bytes=12 * 1024 * 1024)
    own, send, keep = pl.pallas_call(
        gather_kernel,
        name="gather",
        out_shape=(sds(6 * SLOTS), sds(6 * SLOTS + 2), sds(3)),
        in_specs=[pl.BlockSpec(memory_space=pltpu.HBM)] * 9,
        out_specs=(vmem(), vmem(), vmem()),
        scratch_shapes=[pltpu.SMEM((BLOCKS,), jnp.int32)] * 2
        + [pltpu.VMEM((BLOCKS,) + tile, F32)] * 6
        + [pltpu.VMEM((BLOCKS,) + tile, jnp.int32), pltpu.SMEM((MOST + 1,), jnp.int32), pltpu.SemaphoreType.DMA((9,))],
        compiler_params=params,
    )(*[
        pltpu.with_memory_space_constraint(x, pltpu.HBM)
        for x in (covered, reinit, velocity, cot_velocity, stress, cot_stress, forcing, thickness, switch)
    ])
    got = lax.ppermute(send, "ocean", [(0, 1), (1, 0)])
    halves = pl.pallas_call(
        split_kernel,
        name="split",
        out_shape=jax.ShapeDtypeStruct((4, ROWS, ROWS), BF16),
        in_specs=[vmem()],
        out_specs=vmem(),
        compiler_params=params,
    )(kernel)
    packed, kept = pl.pallas_call(
        pack_kernel,
        name="pack",
        out_shape=(jax.ShapeDtypeStruct((ICE, 24, 128), F32), sds()),
        in_specs=[vmem()] * 3,
        out_specs=(vmem(), vmem()),
        compiler_params=params,
    )(own, got, keep)
    arrived = lax.all_to_all(packed, "ice", split_axis=0, concat_axis=0, tiled=True)
    col = pltpu.VMEM((GROUPS,) + tile, F32)
    result = pl.pallas_call(
        work_kernel,
        name="work",
        out_shape=sds(ICE),
        in_specs=[vmem()] * 3,
        out_specs=vmem(),
        scratch_shapes=[col] * 7
        + [
            pltpu.VMEM((HALF, GROUPS) + tile, F32),
            pltpu.VMEM((2 * HALF,) + tile, F32),
            pltpu.VMEM((ROWS, 128), F32),
        ],
        compiler_params=params,
    )(arrived, halves, kept)
    back = lax.all_to_all(result, "ice", split_axis=0, concat_axis=0, tiled=True)
    far = lax.ppermute(back, "ocean", [(0, 1), (1, 0)])
    near, index = pl.pallas_call(
        near_kernel,
        name="near",
        out_shape=(sds(4, BLOCKS + 1), jax.ShapeDtypeStruct((MOST + 1,), jnp.int32)),
        in_specs=[smem(), vmem(), vmem()],
        out_specs=(vmem(), smem()),
        compiler_params=params,
    )(covered, back, switch)
    outs = pl.pallas_call(
        far_kernel,
        name="far",
        out_shape=(sds(BLOCKS),) * 4 + (sds(4, BLOCKS + 1),),
        in_specs=[smem()] + [vmem()] * 3,
        out_specs=(pl.BlockSpec(memory_space=pltpu.HBM),) * 4 + (vmem(),),
        scratch_shapes=[pltpu.SemaphoreType.DMA((4,))],
        input_output_aliases={3: 4},
        compiler_params=params,
    )(index, far, switch, near)
    return outs[:4]


def solution(mesh):
    cells = P("ocean", "ice", None)
    return jax.shard_map(
        shards,
        mesh=mesh,
        in_specs=(cells, cells, cells, cells, cells, P("ocean"), P("ocean"), cells, cells, P()),
        out_specs=(cells, cells, cells, cells),
        check_vma=False,
    )
```

```python
import jax
import jax.numpy as jnp
from jax import lax
from jax.experimental import pallas as pl
from jax.experimental.pallas import tpu as pltpu
from jax.sharding import PartitionSpec as P

PLASTIC = 0.25
VISCOUS = 1.0
GAMMA = 0.6
BETA = 0.9
STEP = 0.04

HALF = 8
BLOCKS = 64
ICE = 64
SLOTS = 16
PARTS = 4
GROUPS = 64
ROWS = 512
MOST = 31
F32 = jnp.float32
BF16 = jnp.bfloat16


def vmem():
    return pl.BlockSpec(memory_space=pltpu.VMEM)


def smem():
    return pl.BlockSpec(memory_space=pltpu.SMEM)


def ranked(covered_ref, index_ref, empty):
    for k in range(MOST + 1):
        index_ref[k] = empty
    count = jnp.int32(0)
    for b in range(BLOCKS):
        flag = covered_ref[b]
        index_ref[jnp.where(flag == 1, count, MOST)] = b
        count = count + flag
    return count


def gather_kernel(
    covered_hbm, reinit_hbm, velo_hbm, cotu_hbm, stress_hbm, cots_hbm, force_hbm, thick_hbm, switch_hbm,
    own_ref, send_ref, keep_ref,
    covered_ref, reinit_ref, velo_ref, cotu_ref, stress_ref, cots_ref, force_ref, thick_ref, switch_ref,
    index_ref, sems,
):
    sources = (covered_hbm, reinit_hbm, velo_hbm, cotu_hbm, stress_hbm, cots_hbm, force_hbm, thick_hbm, switch_hbm)
    targets = (covered_ref, reinit_ref, velo_ref, cotu_ref, stress_ref, cots_ref, force_ref, thick_ref, switch_ref)
    copies = [pltpu.make_async_copy(a, b, sems.at[i]) for i, (a, b) in enumerate(zip(sources, targets))]
    for copy in copies:
        copy.start()
    copies[0].wait()
    heavy = ranked(covered_ref, index_ref, 0) > 1
    sent = [index_ref[jnp.where(heavy, SLOTS + k, 0)] for k in range(SLOTS - 1)]
    owned = [index_ref[jnp.where(heavy, k, 0)] for k in range(SLOTS)]
    places = [(send_ref, k, block) for k, block in enumerate(sent)] + [(own_ref, k, block) for k, block in enumerate(owned)]
    keep_ref[2] = jnp.full((8, 128), heavy.astype(jnp.int32), jnp.int32).astype(F32)
    copies[1].wait()
    for out_ref, k, block in places:
        row = jnp.full((1, 128), 1 - reinit_ref[block], jnp.int32).astype(F32)
        if out_ref is send_ref:
            send_ref[6 * SLOTS + k // 8, k % 8 : k % 8 + 1, :] = row
        else:
            keep_ref[k // 8, k % 8 : k % 8 + 1, :] = row
    for f in range(5):
        copies[2 + f].wait()
        for out_ref, k, block in places:
            out_ref[6 * k + f] = targets[2 + f][block]
    copies[7].wait()
    copies[8].wait()
    for out_ref, k, block in places:
        coef = jnp.where(switch_ref[block] == 1, PLASTIC, VISCOUS)
        out_ref[6 * k + 5] = thick_ref[block] * coef


def split(x):
    high = x.astype(BF16)
    return high, (x - high.astype(F32)).astype(BF16)


def split_kernel(kernel_ref, halves_ref):
    whole = kernel_ref[...]
    halves_ref[0], halves_ref[1] = split(whole)
    halves_ref[2], halves_ref[3] = split(whole.T)


def pack_kernel(own_ref, got_ref, keep_ref, packed_hbm, kept_ref, out_ref, sems):
    heavy = keep_ref[2] > 0.5
    lane = lax.broadcasted_iota(jnp.int32, (8, 128), 1)
    low = lane < 64
    spot = lane % 64

    copies = []
    for k in range(SLOTS):
        tiles = [own_ref[6 * k + f] for f in range(6)]
        if k < SLOTS - 1:
            tiles = [jnp.where(heavy, tile, got_ref[6 * k + f]) for f, tile in enumerate(tiles)]
        for q in range(PARTS):
            shift = (16 - 32 * q) % 128
            for t in range(3):
                both = jnp.where(
                    low,
                    pltpu.roll(tiles[2 * t], shift, 1) if shift else tiles[2 * t],
                    pltpu.roll(tiles[2 * t + 1], (shift + 64) % 128, 1),
                )
                if q == 0:
                    both = jnp.where(spot >= 16, both, 0.0)
                if q == PARTS - 1:
                    both = jnp.where(spot < 48, both, 0.0)
                out_ref[PARTS * k + q, pl.ds(8 * t, 8), :] = both
        if k % 4 == 3:
            rows = pl.ds(PARTS * (k - 3), 4 * PARTS)
            copies.append(pltpu.make_async_copy(out_ref.at[rows], packed_hbm.at[rows], sems.at[k // 4]))
            copies[-1].start()
    slot = lax.axis_index("ice") // PARTS
    sub = slot % 8
    mine = jnp.broadcast_to(keep_ref[slot // 8, pl.ds(sub, 1), :], (8, 128))
    other = jnp.broadcast_to(got_ref[6 * SLOTS + slot // 8, pl.ds(sub, 1), :], (8, 128))
    own_slot = jnp.full((8, 128), slot, jnp.int32) == SLOTS - 1
    kept_ref[...] = jnp.where(jnp.logical_or(heavy, own_slot), mine, other)
    for copy in copies:
        copy.wait()


def product(a_high, a_low, b):
    b_high, b_low = split(b)

    def dot(x, y):
        return jnp.dot(x, y, preferred_element_type=F32)

    wide = dot(a_high, jnp.concatenate([b_high, b_low], axis=1))
    return (dot(a_low, b_high) + wide[:, 128:]) + wide[:, :128]


def spread(v):
    return pl.ds(v, 8, stride=GROUPS)


def work_kernel(
    in_ref, halves_ref, kept_ref, out_ref,
    x_ref, y_ref, zf_ref, zb_ref, f_ref, acc_ref, af_ref, saved_ref, coef_ref, col_ref,
):
    part = lax.axis_index("ice") % PARTS
    lane = lax.broadcasted_iota(jnp.int32, (8, 128), 1)
    sub = lax.broadcasted_iota(jnp.int32, (8, 128), 0)
    low = lane < 64
    edge = jnp.logical_and(lane % 64 == 16, part == 0)

    last = in_ref[:, 16:24, :].reshape(ROWS, 128)
    col_ref[...] = product(halves_ref[0], halves_ref[1], last)

    def load(v, t):
        return in_ref[pl.ds(v // 8, 8, stride=8), 8 * t + v % 8, :]

    for v in range(GROUPS):
        zeta = col_ref[spread(v), :]
        zb_ref[v] = jnp.where(low, -STEP, zeta)
        zf_ref[v] = jnp.where(low, pltpu.roll(zeta, 64, 1), -STEP)
        x_ref[v] = load(v, 0)
        y_ref[v] = load(v, 1)
        f_ref[v] = jnp.where(low, STEP * load(v, 2), 0.0)
        af_ref[v] = jnp.zeros((8, 128), F32)
        acc_ref[v] = jnp.zeros((8, 128), F32)

    gamma = jnp.full((8, 128), GAMMA, F32)
    for j in range(2 * HALF):
        coef_ref[j] = gamma
    coef_ref[0] = jnp.where(low, GAMMA, 1.0)
    coef_ref[HALF] = GAMMA * kept_ref[...]

    def subcycle(j, late):
        coef = coef_ref[j]
        above = jnp.where(sub == 0, 0.0, pltpu.roll(x_ref[GROUPS - 1], 1, 0))
        first_p = None
        held = None
        for v in range(GROUPS + 1):
            if v < GROUPS:
                x = x_ref[v]
                left = jnp.where(edge, 0.0, pltpu.roll(x, 1, 1))
                strain = 2.0 * x - (above + left)
                y = coef * y_ref[v] + zf_ref[v] * strain
                p = zb_ref[v] * y
                both = jnp.where(low, strain, y)
                if late:
                    acc_ref[v] += both * pltpu.roll(saved_ref[2 * HALF - 1 - j, v], 64, 1)
                else:
                    saved_ref[j, v] = both
                y_ref[v] = y
                af_ref[v] += x
                above = x
                if v == 0:
                    first_p = p
                below = p
            else:
                below = jnp.where(sub == 7, 0.0, pltpu.roll(first_p, 7, 0))
            if v > 0:
                old_x, old_p = held
                right = pltpu.roll(old_p, 127, 1)
                x_ref[v - 1] = BETA * old_x + (2.0 * old_p - (below + right)) + f_ref[v - 1]
            held = (x, p)

    for j in range(2 * HALF):
        subcycle(j, j >= HALF)

    for v in range(GROUPS):
        total = acc_ref[v]
        col_ref[spread(v), :] = total + pltpu.roll(total, 64, 1)
    adj_q = product(halves_ref[2], halves_ref[3], col_ref[...])
    turn = [lax.rem(32 * (f + part) + 48, 128) for f in range(4)]
    field = lax.rem(lane // 32 + (PARTS - part), PARTS)
    for v in range(GROUPS):
        tile = jnp.where(
            field == 0,
            pltpu.roll(x_ref[v], turn[0], 1),
            jnp.where(
                field == 1, GAMMA * pltpu.roll(y_ref[v], turn[1], 1), STEP * pltpu.roll(af_ref[v], turn[3], 1)
            ),
        )
        col_ref[spread(v), :] = tile
    moved = pltpu.roll(adj_q, turn[2], 1).reshape(GROUPS, 8, 128)
    result = jnp.where((field == 2)[None], moved, col_ref[...].reshape(GROUPS, 8, 128))
    out_ref[...] = result


def unpack(back_ref, switch_ref, all_ref, f, base, block):
    lane = lax.broadcasted_iota(jnp.int32, (8, 128), 1)
    whole = back_ref[base + (-f) % PARTS]
    for g in range(1, PARTS):
        whole = jnp.where(lane >= 32 * g, back_ref[base + (g - f) % PARTS], whole)
    if f:
        whole = pltpu.roll(whole, 128 - 32 * f, 1)
    if f == 2:
        inside = jnp.minimum(block, BLOCKS - 1)
        whole = whole * jnp.where(switch_ref[inside] == 1, PLASTIC, VISCOUS)
    all_ref[f, block] = whole


def near_kernel(covered_ref, back_ref, switch_ref, all_ref, index_ref):
    heavy = ranked(covered_ref, index_ref, BLOCKS) > 1
    blocks = [index_ref[r] for r in range(SLOTS)]
    for f in range(4):
        all_ref[f] = jnp.zeros(all_ref.shape[1:], F32)
        for r, block in enumerate(blocks):
            base = jnp.where(heavy, PARTS * r, PARTS * (SLOTS - 1))
            unpack(back_ref, switch_ref, all_ref, f, base, block)


def far_kernel(index_ref, far_ref, switch_ref, near_ref, gu_hbm, gs_hbm, gq_hbm, gf_hbm, all_ref, sems):
    copies = []
    for f, ref in ((0, gu_hbm), (1, gs_hbm), (3, gf_hbm), (2, gq_hbm)):
        for r in range(SLOTS, MOST):
            unpack(far_ref, switch_ref, all_ref, f, PARTS * (r - SLOTS), index_ref[r])
        copy = pltpu.make_async_copy(all_ref.at[f, pl.ds(0, BLOCKS)], ref, sems.at[f])
        copy.start()
        copies.append(copy)
    for copy in copies:
        copy.wait()


def shards(velocity, stress, thickness, forcing, switch, covered, reinit, cot_velocity, cot_stress, kernel):
    tile = (8, 128)

    def sds(*lead):
        return jax.ShapeDtypeStruct(lead + tile, F32)

    params = pltpu.CompilerParams(vmem_limit_bytes=12 * 1024 * 1024)
    own, send, keep = pl.pallas_call(
        gather_kernel,
        name="gather",
        out_shape=(sds(6 * SLOTS), sds(6 * SLOTS + 2), sds(3)),
        in_specs=[pl.BlockSpec(memory_space=pltpu.HBM)] * 9,
        out_specs=(vmem(), vmem(), vmem()),
        scratch_shapes=[pltpu.SMEM((BLOCKS,), jnp.int32)] * 2
        + [pltpu.VMEM((BLOCKS,) + tile, F32)] * 6
        + [pltpu.VMEM((BLOCKS,) + tile, jnp.int32), pltpu.SMEM((MOST + 1,), jnp.int32), pltpu.SemaphoreType.DMA((9,))],
        compiler_params=params,
    )(*[
        pltpu.with_memory_space_constraint(x, pltpu.HBM)
        for x in (covered, reinit, velocity, cot_velocity, stress, cot_stress, forcing, thickness, switch)
    ])
    got = lax.ppermute(send, "ocean", [(0, 1), (1, 0)])
    halves = pl.pallas_call(
        split_kernel,
        name="split",
        out_shape=jax.ShapeDtypeStruct((4, ROWS, ROWS), BF16),
        in_specs=[vmem()],
        out_specs=vmem(),
        compiler_params=params,
    )(kernel)
    packed, kept = pl.pallas_call(
        pack_kernel,
        name="pack",
        out_shape=(jax.ShapeDtypeStruct((ICE, 24, 128), F32), sds()),
        in_specs=[vmem()] * 3,
        out_specs=(pl.BlockSpec(memory_space=pltpu.HBM), vmem()),
        scratch_shapes=[pltpu.VMEM((ICE, 24, 128), F32), pltpu.SemaphoreType.DMA((4,))],
        compiler_params=params,
    )(own, got, keep)
    arrived = lax.all_to_all(packed, "ice", split_axis=0, concat_axis=0, tiled=True)
    col = pltpu.VMEM((GROUPS,) + tile, F32)
    result = pl.pallas_call(
        work_kernel,
        name="work",
        out_shape=sds(ICE),
        in_specs=[vmem()] * 3,
        out_specs=vmem(),
        scratch_shapes=[col] * 7
        + [
            pltpu.VMEM((HALF, GROUPS) + tile, F32),
            pltpu.VMEM((2 * HALF,) + tile, F32),
            pltpu.VMEM((ROWS, 128), F32),
        ],
        compiler_params=params,
    )(arrived, halves, kept)
    back = lax.all_to_all(result, "ice", split_axis=0, concat_axis=0, tiled=True)
    far = lax.ppermute(back, "ocean", [(0, 1), (1, 0)])
    near, index = pl.pallas_call(
        near_kernel,
        name="near",
        out_shape=(sds(4, BLOCKS + 1), jax.ShapeDtypeStruct((MOST + 1,), jnp.int32)),
        in_specs=[smem(), vmem(), vmem()],
        out_specs=(vmem(), smem()),
        compiler_params=params,
    )(covered, back, switch)
    outs = pl.pallas_call(
        far_kernel,
        name="far",
        out_shape=(sds(BLOCKS),) * 4 + (sds(4, BLOCKS + 1),),
        in_specs=[smem()] + [vmem()] * 3,
        out_specs=(pl.BlockSpec(memory_space=pltpu.HBM),) * 4 + (vmem(),),
        scratch_shapes=[pltpu.SemaphoreType.DMA((4,))],
        input_output_aliases={3: 4},
        compiler_params=params,
    )(index, far, switch, near)
    return outs[:4]


def solution(mesh):
    cells = P("ocean", "ice", None)
    return jax.shard_map(
        shards,
        mesh=mesh,
        in_specs=(cells, cells, cells, cells, cells, P("ocean"), P("ocean"), cells, cells, P()),
        out_specs=(cells, cells, cells, cells),
        check_vma=False,
    )
```

```python
import jax
import jax.numpy as jnp
from jax import lax
from jax.experimental import pallas as pl
from jax.experimental.pallas import tpu as pltpu
from jax.sharding import PartitionSpec as P

PLASTIC = 0.25
VISCOUS = 1.0
GAMMA = 0.6
BETA = 0.9
STEP = 0.04

HALF = 8
BLOCKS = 64
ICE = 64
SLOTS = 16
PARTS = 4
GROUPS = 64
ROWS = 512
MOST = 31
F32 = jnp.float32
BF16 = jnp.bfloat16


def vmem():
    return pl.BlockSpec(memory_space=pltpu.VMEM)


def smem():
    return pl.BlockSpec(memory_space=pltpu.SMEM)


def ranked(covered_ref, index_ref, empty):
    for k in range(MOST + 1):
        index_ref[k] = empty
    count = jnp.int32(0)
    for b in range(BLOCKS):
        flag = covered_ref[b]
        index_ref[jnp.where(flag == 1, count, MOST)] = b
        count = count + flag
    return count


def gather_kernel(
    covered_hbm, reinit_hbm, velo_hbm, cotu_hbm, stress_hbm, cots_hbm, force_hbm, thick_hbm, switch_hbm,
    own_ref, send_ref, keep_ref,
    covered_ref, reinit_ref, velo_ref, cotu_ref, stress_ref, cots_ref, force_ref, thick_ref, switch_ref,
    index_ref, sems,
):
    sources = (covered_hbm, reinit_hbm, velo_hbm, cotu_hbm, stress_hbm, cots_hbm, force_hbm, thick_hbm, switch_hbm)
    targets = (covered_ref, reinit_ref, velo_ref, cotu_ref, stress_ref, cots_ref, force_ref, thick_ref, switch_ref)
    copies = [pltpu.make_async_copy(a, b, sems.at[i]) for i, (a, b) in enumerate(zip(sources, targets))]
    for copy in copies:
        copy.start()
    copies[0].wait()
    heavy = ranked(covered_ref, index_ref, 0) > 1
    sent = [index_ref[jnp.where(heavy, SLOTS + k, 0)] for k in range(SLOTS - 1)]
    owned = [index_ref[jnp.where(heavy, k, 0)] for k in range(SLOTS)]
    places = [(send_ref, k, block) for k, block in enumerate(sent)] + [(own_ref, k, block) for k, block in enumerate(owned)]
    keep_ref[2] = jnp.full((8, 128), heavy.astype(jnp.int32), jnp.int32).astype(F32)
    copies[1].wait()
    for out_ref, k, block in places:
        row = jnp.full((1, 128), 1 - reinit_ref[block], jnp.int32).astype(F32)
        if out_ref is send_ref:
            send_ref[6 * SLOTS + k // 8, k % 8 : k % 8 + 1, :] = row
        else:
            keep_ref[k // 8, k % 8 : k % 8 + 1, :] = row
    for f in range(5):
        copies[2 + f].wait()
        for out_ref, k, block in places:
            out_ref[6 * k + f] = targets[2 + f][block]
    copies[7].wait()
    copies[8].wait()
    for out_ref, k, block in places:
        coef = jnp.where(switch_ref[block] == 1, PLASTIC, VISCOUS)
        out_ref[6 * k + 5] = thick_ref[block] * coef


def split(x):
    high = x.astype(BF16)
    return high, (x - high.astype(F32)).astype(BF16)


def split_kernel(kernel_ref, halves_ref):
    whole = kernel_ref[...]
    halves_ref[0], halves_ref[1] = split(whole)
    halves_ref[2], halves_ref[3] = split(whole.T)


def pack(fields_ref, slots, packed_hbm, out_ref, sems):
    lane = lax.broadcasted_iota(jnp.int32, (8, 128), 1)
    low = lane < 64
    spot = lane % 64
    copies = []
    sent = 0
    for k in range(slots):
        tiles = [fields_ref[6 * k + f] for f in range(6)]
        for q in range(PARTS):
            shift = (16 - 32 * q) % 128
            for t in range(3):
                both = jnp.where(
                    low, pltpu.roll(tiles[2 * t], shift, 1), pltpu.roll(tiles[2 * t + 1], (shift + 64) % 128, 1)
                )
                if q == 0:
                    both = jnp.where(spot >= 16, both, 0.0)
                if q == PARTS - 1:
                    both = jnp.where(spot < 48, both, 0.0)
                out_ref[PARTS * k + q, pl.ds(8 * t, 8), :] = both
        if k % 4 == 3 or k == slots - 1:
            rows = pl.ds(PARTS * sent, PARTS * (k + 1 - sent))
            copies.append(pltpu.make_async_copy(out_ref.at[rows], packed_hbm.at[rows], sems.at[k // 4]))
            copies[-1].start()
            sent = k + 1
    for copy in copies:
        copy.wait()


def pack_own_kernel(own_ref, packed_hbm, out_ref, sems):
    pack(own_ref, SLOTS, packed_hbm, out_ref, sems)


def pack_got_kernel(got_ref, keep_ref, own_hbm, packed_hbm, kept_ref, out_ref, sems):
    heavy = keep_ref[2] > 0.5
    slot = lax.axis_index("ice") // PARTS
    sub = slot % 8
    mine = jnp.broadcast_to(keep_ref[slot // 8, pl.ds(sub, 1), :], (8, 128))
    other = jnp.broadcast_to(got_ref[6 * SLOTS + slot // 8, pl.ds(sub, 1), :], (8, 128))
    own_slot = jnp.full((8, 128), slot, jnp.int32) == SLOTS - 1
    kept_ref[...] = jnp.where(jnp.logical_or(heavy, own_slot), mine, other)

    @pl.when(jnp.max(keep_ref[2]) < 0.5)
    def light():
        pack(got_ref, SLOTS - 1, packed_hbm, out_ref, sems)


def product(a_high, a_low, b):
    b_high, b_low = split(b)

    def dot(x, y):
        return jnp.dot(x, y, preferred_element_type=F32)

    wide = dot(a_high, jnp.concatenate([b_high, b_low], axis=1))
    return (dot(a_low, b_high) + wide[:, 128:]) + wide[:, :128]


def spread(v):
    return pl.ds(v, 8, stride=GROUPS)


def work_kernel(
    in_ref, halves_ref, kept_ref, out_ref,
    x_ref, y_ref, zf_ref, zb_ref, f_ref, acc_ref, af_ref, saved_ref, coef_ref, col_ref,
):
    part = lax.axis_index("ice") % PARTS
    lane = lax.broadcasted_iota(jnp.int32, (8, 128), 1)
    sub = lax.broadcasted_iota(jnp.int32, (8, 128), 0)
    low = lane < 64
    edge = jnp.logical_and(lane % 64 == 16, part == 0)

    last = in_ref[:, 16:24, :].reshape(ROWS, 128)
    col_ref[...] = product(halves_ref[0], halves_ref[1], last)

    def load(v, t):
        return in_ref[pl.ds(v // 8, 8, stride=8), 8 * t + v % 8, :]

    for v in range(GROUPS):
        zeta = col_ref[spread(v), :]
        zb_ref[v] = jnp.where(low, -STEP, zeta)
        zf_ref[v] = jnp.where(low, pltpu.roll(zeta, 64, 1), -STEP)
        x_ref[v] = load(v, 0)
        y_ref[v] = load(v, 1)
        f_ref[v] = jnp.where(low, STEP * load(v, 2), 0.0)
        af_ref[v] = jnp.zeros((8, 128), F32)
        acc_ref[v] = jnp.zeros((8, 128), F32)

    gamma = jnp.full((8, 128), GAMMA, F32)
    for j in range(2 * HALF):
        coef_ref[j] = gamma
    coef_ref[0] = jnp.where(low, GAMMA, 1.0)
    coef_ref[HALF] = GAMMA * kept_ref[...]

    def subcycle(j, late):
        coef = coef_ref[j]
        above = jnp.where(sub == 0, 0.0, pltpu.roll(x_ref[GROUPS - 1], 1, 0))
        first_p = None
        held = None
        for v in range(GROUPS + 1):
            if v < GROUPS:
                x = x_ref[v]
                left = jnp.where(edge, 0.0, pltpu.roll(x, 1, 1))
                strain = 2.0 * x - (above + left)
                y = coef * y_ref[v] + zf_ref[v] * strain
                p = zb_ref[v] * y
                both = jnp.where(low, strain, y)
                if late:
                    acc_ref[v] += both * pltpu.roll(saved_ref[2 * HALF - 1 - j, v], 64, 1)
                else:
                    saved_ref[j, v] = both
                y_ref[v] = y
                af_ref[v] += x
                above = x
                if v == 0:
                    first_p = p
                below = p
            else:
                below = jnp.where(sub == 7, 0.0, pltpu.roll(first_p, 7, 0))
            if v > 0:
                old_x, old_p = held
                right = pltpu.roll(old_p, 127, 1)
                x_ref[v - 1] = BETA * old_x + (2.0 * old_p - (below + right)) + f_ref[v - 1]
            held = (x, p)

    for j in range(2 * HALF):
        subcycle(j, j >= HALF)

    for v in range(GROUPS):
        total = acc_ref[v]
        col_ref[spread(v), :] = total + pltpu.roll(total, 64, 1)
    adj_q = product(halves_ref[2], halves_ref[3], col_ref[...])
    turn = [lax.rem(32 * (f + part) + 48, 128) for f in range(4)]
    field = lax.rem(lane // 32 + (PARTS - part), PARTS)
    for v in range(GROUPS):
        tile = jnp.where(
            field == 0,
            pltpu.roll(x_ref[v], turn[0], 1),
            jnp.where(
                field == 1, GAMMA * pltpu.roll(y_ref[v], turn[1], 1), STEP * pltpu.roll(af_ref[v], turn[3], 1)
            ),
        )
        col_ref[spread(v), :] = tile
    moved = pltpu.roll(adj_q, turn[2], 1).reshape(GROUPS, 8, 128)
    result = jnp.where((field == 2)[None], moved, col_ref[...].reshape(GROUPS, 8, 128))
    out_ref[...] = result


def unpack(back_ref, switch_ref, all_ref, f, base, block):
    lane = lax.broadcasted_iota(jnp.int32, (8, 128), 1)
    whole = back_ref[base + (-f) % PARTS]
    for g in range(1, PARTS):
        whole = jnp.where(lane >= 32 * g, back_ref[base + (g - f) % PARTS], whole)
    if f:
        whole = pltpu.roll(whole, 128 - 32 * f, 1)
    if f == 2:
        inside = jnp.minimum(block, BLOCKS - 1)
        whole = whole * jnp.where(switch_ref[inside] == 1, PLASTIC, VISCOUS)
    all_ref[f, block] = whole


def near_kernel(covered_ref, back_ref, switch_ref, all_ref, index_ref):
    heavy = ranked(covered_ref, index_ref, BLOCKS) > 1
    blocks = [index_ref[r] for r in range(SLOTS)]
    for f in range(4):
        all_ref[f] = jnp.zeros(all_ref.shape[1:], F32)
        for r, block in enumerate(blocks):
            base = jnp.where(heavy, PARTS * r, PARTS * (SLOTS - 1))
            unpack(back_ref, switch_ref, all_ref, f, base, block)


def far_kernel(index_ref, far_ref, switch_ref, near_ref, gu_hbm, gs_hbm, gq_hbm, gf_hbm, all_ref, sems):
    copies = []
    for f, ref in ((0, gu_hbm), (1, gs_hbm), (3, gf_hbm), (2, gq_hbm)):
        for r in range(SLOTS, MOST):
            unpack(far_ref, switch_ref, all_ref, f, PARTS * (r - SLOTS), index_ref[r])
        copy = pltpu.make_async_copy(all_ref.at[f, pl.ds(0, BLOCKS)], ref, sems.at[f])
        copy.start()
        copies.append(copy)
    for copy in copies:
        copy.wait()


def shards(velocity, stress, thickness, forcing, switch, covered, reinit, cot_velocity, cot_stress, kernel):
    tile = (8, 128)

    def sds(*lead):
        return jax.ShapeDtypeStruct(lead + tile, F32)

    params = pltpu.CompilerParams(vmem_limit_bytes=12 * 1024 * 1024)
    own, send, keep = pl.pallas_call(
        gather_kernel,
        name="gather",
        out_shape=(sds(6 * SLOTS), sds(6 * SLOTS + 2), sds(3)),
        in_specs=[pl.BlockSpec(memory_space=pltpu.HBM)] * 9,
        out_specs=(vmem(), vmem(), vmem()),
        scratch_shapes=[pltpu.SMEM((BLOCKS,), jnp.int32)] * 2
        + [pltpu.VMEM((BLOCKS,) + tile, F32)] * 6
        + [pltpu.VMEM((BLOCKS,) + tile, jnp.int32), pltpu.SMEM((MOST + 1,), jnp.int32), pltpu.SemaphoreType.DMA((9,))],
        compiler_params=params,
    )(*[
        pltpu.with_memory_space_constraint(x, pltpu.HBM)
        for x in (covered, reinit, velocity, cot_velocity, stress, cot_stress, forcing, thickness, switch)
    ])
    got = lax.ppermute(send, "ocean", [(0, 1), (1, 0)])
    halves = pl.pallas_call(
        split_kernel,
        name="split",
        out_shape=jax.ShapeDtypeStruct((4, ROWS, ROWS), BF16),
        in_specs=[vmem()],
        out_specs=vmem(),
        compiler_params=params,
    )(kernel)
    windows = jax.ShapeDtypeStruct((ICE, 24, 128), F32)
    hbm = pl.BlockSpec(memory_space=pltpu.HBM)
    staging = [pltpu.VMEM((ICE, 24, 128), F32), pltpu.SemaphoreType.DMA((4,))]
    packed = pl.pallas_call(
        pack_own_kernel,
        name="pack_own",
        out_shape=windows,
        in_specs=[vmem()],
        out_specs=hbm,
        scratch_shapes=staging,
        compiler_params=params,
    )(own)
    packed, kept = pl.pallas_call(
        pack_got_kernel,
        name="pack_got",
        out_shape=(windows, sds()),
        in_specs=[vmem(), vmem(), hbm],
        out_specs=(hbm, vmem()),
        scratch_shapes=staging,
        input_output_aliases={2: 0},
        compiler_params=params,
    )(got, keep, packed)
    arrived = lax.all_to_all(packed, "ice", split_axis=0, concat_axis=0, tiled=True)
    col = pltpu.VMEM((GROUPS,) + tile, F32)
    result = pl.pallas_call(
        work_kernel,
        name="work",
        out_shape=sds(ICE),
        in_specs=[vmem()] * 3,
        out_specs=vmem(),
        scratch_shapes=[col] * 7
        + [
            pltpu.VMEM((HALF, GROUPS) + tile, F32),
            pltpu.VMEM((2 * HALF,) + tile, F32),
            pltpu.VMEM((ROWS, 128), F32),
        ],
        compiler_params=params,
    )(arrived, halves, kept)
    back = lax.all_to_all(result, "ice", split_axis=0, concat_axis=0, tiled=True)
    far = lax.ppermute(back, "ocean", [(0, 1), (1, 0)])
    near, index = pl.pallas_call(
        near_kernel,
        name="near",
        out_shape=(sds(4, BLOCKS + 1), jax.ShapeDtypeStruct((MOST + 1,), jnp.int32)),
        in_specs=[smem(), vmem(), vmem()],
        out_specs=(vmem(), smem()),
        compiler_params=params,
    )(covered, back, switch)
    outs = pl.pallas_call(
        far_kernel,
        name="far",
        out_shape=(sds(BLOCKS),) * 4 + (sds(4, BLOCKS + 1),),
        in_specs=[smem()] + [vmem()] * 3,
        out_specs=(pl.BlockSpec(memory_space=pltpu.HBM),) * 4 + (vmem(),),
        scratch_shapes=[pltpu.SemaphoreType.DMA((4,))],
        input_output_aliases={3: 4},
        compiler_params=params,
    )(index, far, switch, near)
    return outs[:4]


def solution(mesh):
    cells = P("ocean", "ice", None)
    return jax.shard_map(
        shards,
        mesh=mesh,
        in_specs=(cells, cells, cells, cells, cells, P("ocean"), P("ocean"), cells, cells, P()),
        out_specs=(cells, cells, cells, cells),
        check_vma=False,
    )
```

```python
import jax
import jax.numpy as jnp
from jax import lax
from jax.experimental import pallas as pl
from jax.experimental.pallas import tpu as pltpu
from jax.sharding import PartitionSpec as P

PLASTIC = 0.25
VISCOUS = 1.0
GAMMA = 0.6
BETA = 0.9
STEP = 0.04

HALF = 8
BLOCKS = 64
ICE = 64
SLOTS = 16
PARTS = 4
GROUPS = 64
ROWS = 512
MOST = 31
F32 = jnp.float32
BF16 = jnp.bfloat16


def vmem():
    return pl.BlockSpec(memory_space=pltpu.VMEM)


def smem():
    return pl.BlockSpec(memory_space=pltpu.SMEM)


def ranked(covered_ref, index_ref, empty):
    for k in range(MOST + 1):
        index_ref[k] = empty
    count = jnp.int32(0)
    for b in range(BLOCKS):
        flag = covered_ref[b]
        index_ref[jnp.where(flag == 1, count, MOST)] = b
        count = count + flag
    return count


def gather_kernel(
    covered_hbm, reinit_hbm, velo_hbm, cotu_hbm, stress_hbm, cots_hbm, force_hbm, thick_hbm, switch_hbm,
    own_ref, send_ref, keep_ref,
    covered_ref, reinit_ref, velo_ref, cotu_ref, stress_ref, cots_ref, force_ref, thick_ref, switch_ref,
    index_ref, sems,
):
    sources = (covered_hbm, reinit_hbm, velo_hbm, cotu_hbm, stress_hbm, cots_hbm, force_hbm, thick_hbm, switch_hbm)
    targets = (covered_ref, reinit_ref, velo_ref, cotu_ref, stress_ref, cots_ref, force_ref, thick_ref, switch_ref)
    copies = [pltpu.make_async_copy(a, b, sems.at[i]) for i, (a, b) in enumerate(zip(sources, targets))]
    for copy in copies:
        copy.start()
    copies[0].wait()
    heavy = ranked(covered_ref, index_ref, 0) > 1
    sent = [index_ref[jnp.where(heavy, SLOTS + k, 0)] for k in range(SLOTS - 1)]
    owned = [index_ref[jnp.where(heavy, k, 0)] for k in range(SLOTS)]
    places = [(send_ref, k, block) for k, block in enumerate(sent)] + [(own_ref, k, block) for k, block in enumerate(owned)]
    keep_ref[2] = jnp.full((8, 128), heavy.astype(jnp.int32), jnp.int32).astype(F32)
    copies[1].wait()
    for out_ref, k, block in places:
        row = jnp.full((1, 128), 1 - reinit_ref[block], jnp.int32).astype(F32)
        if out_ref is send_ref:
            send_ref[6 * SLOTS + k // 8, k % 8 : k % 8 + 1, :] = row
        else:
            keep_ref[k // 8, k % 8 : k % 8 + 1, :] = row
    for f in range(5):
        copies[2 + f].wait()
        for out_ref, k, block in places:
            out_ref[6 * k + f] = targets[2 + f][block]
    copies[7].wait()
    copies[8].wait()
    for out_ref, k, block in places:
        coef = jnp.where(switch_ref[block] == 1, PLASTIC, VISCOUS)
        out_ref[6 * k + 5] = thick_ref[block] * coef


def split(x):
    high = x.astype(BF16)
    return high, (x - high.astype(F32)).astype(BF16)


def pack(fields_ref, slots, out_ref):
    lane = lax.broadcasted_iota(jnp.int32, (8, 128), 1)
    low = lane < 64
    spot = lane % 64
    for k in range(slots):
        tiles = [fields_ref[6 * k + f] for f in range(6)]
        for q in range(PARTS):
            shift = (16 - 32 * q) % 128
            for t in range(3):
                both = jnp.where(
                    low, pltpu.roll(tiles[2 * t], shift, 1), pltpu.roll(tiles[2 * t + 1], (shift + 64) % 128, 1)
                )
                if q == 0:
                    both = jnp.where(spot >= 16, both, 0.0)
                if q == PARTS - 1:
                    both = jnp.where(spot < 48, both, 0.0)
                out_ref[PARTS * k + q, pl.ds(8 * t, 8), :] = both


def pack_own_kernel(own_ref, kernel_hbm, out_ref, halves_ref, kernel_ref, sem):
    copy = pltpu.make_async_copy(kernel_hbm, kernel_ref, sem)
    copy.start()
    pack(own_ref, SLOTS, out_ref)
    copy.wait()
    whole = kernel_ref[...]
    halves_ref[0], halves_ref[1] = split(whole)
    halves_ref[2], halves_ref[3] = split(whole.T)


def pack_got_kernel(got_ref, keep_ref, packed_ref, out_ref, kept_ref):
    heavy = keep_ref[2] > 0.5
    slot = lax.axis_index("ice") // PARTS
    sub = slot % 8
    mine = jnp.broadcast_to(keep_ref[slot // 8, pl.ds(sub, 1), :], (8, 128))
    other = jnp.broadcast_to(got_ref[6 * SLOTS + slot // 8, pl.ds(sub, 1), :], (8, 128))
    own_slot = jnp.full((8, 128), slot, jnp.int32) == SLOTS - 1
    kept_ref[...] = jnp.where(jnp.logical_or(heavy, own_slot), mine, other)

    @pl.when(jnp.max(keep_ref[2]) < 0.5)
    def light():
        pack(got_ref, SLOTS - 1, out_ref)


def product(a_high, a_low, b):
    b_high, b_low = split(b)

    def dot(x, y):
        return jnp.dot(x, y, preferred_element_type=F32)

    wide = dot(a_high, jnp.concatenate([b_high, b_low], axis=1))
    return (dot(a_low, b_high) + wide[:, 128:]) + wide[:, :128]


def spread(v):
    return pl.ds(v, 8, stride=GROUPS)


def work_kernel(
    in_ref, halves_ref, kept_ref, out_ref,
    x_ref, y_ref, zf_ref, zb_ref, f_ref, acc_ref, af_ref, saved_ref, coef_ref, col_ref,
):
    part = lax.axis_index("ice") % PARTS
    lane = lax.broadcasted_iota(jnp.int32, (8, 128), 1)
    sub = lax.broadcasted_iota(jnp.int32, (8, 128), 0)
    low = lane < 64
    edge = jnp.logical_and(lane % 64 == 16, part == 0)

    last = in_ref[:, 16:24, :].reshape(ROWS, 128)
    col_ref[...] = product(halves_ref[0], halves_ref[1], last)

    def load(v, t):
        return in_ref[pl.ds(v // 8, 8, stride=8), 8 * t + v % 8, :]

    for v in range(GROUPS):
        zeta = col_ref[spread(v), :]
        zb_ref[v] = jnp.where(low, -STEP, zeta)
        zf_ref[v] = jnp.where(low, pltpu.roll(zeta, 64, 1), -STEP)
        x_ref[v] = load(v, 0)
        y_ref[v] = load(v, 1)
        f_ref[v] = jnp.where(low, STEP * load(v, 2), 0.0)
        af_ref[v] = jnp.zeros((8, 128), F32)
        acc_ref[v] = jnp.zeros((8, 128), F32)

    gamma = jnp.full((8, 128), GAMMA, F32)
    for j in range(2 * HALF):
        coef_ref[j] = gamma
    coef_ref[0] = jnp.where(low, GAMMA, 1.0)
    coef_ref[HALF] = GAMMA * kept_ref[...]

    def subcycle(j, late):
        coef = coef_ref[j]
        above = jnp.where(sub == 0, 0.0, pltpu.roll(x_ref[GROUPS - 1], 1, 0))
        first_p = None
        held = None
        for v in range(GROUPS + 1):
            if v < GROUPS:
                x = x_ref[v]
                left = jnp.where(edge, 0.0, pltpu.roll(x, 1, 1))
                strain = 2.0 * x - (above + left)
                y = coef * y_ref[v] + zf_ref[v] * strain
                p = zb_ref[v] * y
                both = jnp.where(low, strain, y)
                if late:
                    acc_ref[v] += both * pltpu.roll(saved_ref[2 * HALF - 1 - j, v], 64, 1)
                else:
                    saved_ref[j, v] = both
                y_ref[v] = y
                af_ref[v] += x
                above = x
                if v == 0:
                    first_p = p
                below = p
            else:
                below = jnp.where(sub == 7, 0.0, pltpu.roll(first_p, 7, 0))
            if v > 0:
                old_x, old_p = held
                right = pltpu.roll(old_p, 127, 1)
                x_ref[v - 1] = BETA * old_x + (2.0 * old_p - (below + right)) + f_ref[v - 1]
            held = (x, p)

    for j in range(2 * HALF):
        subcycle(j, j >= HALF)

    for v in range(GROUPS):
        total = acc_ref[v]
        col_ref[spread(v), :] = total + pltpu.roll(total, 64, 1)
    adj_q = product(halves_ref[2], halves_ref[3], col_ref[...])
    turn = [lax.rem(32 * (f + part) + 48, 128) for f in range(4)]
    field = lax.rem(lane // 32 + (PARTS - part), PARTS)
    for v in range(GROUPS):
        tile = jnp.where(
            field == 0,
            pltpu.roll(x_ref[v], turn[0], 1),
            jnp.where(
                field == 1, GAMMA * pltpu.roll(y_ref[v], turn[1], 1), STEP * pltpu.roll(af_ref[v], turn[3], 1)
            ),
        )
        col_ref[spread(v), :] = tile
    moved = pltpu.roll(adj_q, turn[2], 1).reshape(GROUPS, 8, 128)
    result = jnp.where((field == 2)[None], moved, col_ref[...].reshape(GROUPS, 8, 128))
    out_ref[...] = result


def unpack(back_ref, switch_ref, all_ref, f, base, block):
    lane = lax.broadcasted_iota(jnp.int32, (8, 128), 1)
    whole = back_ref[base + (-f) % PARTS]
    for g in range(1, PARTS):
        whole = jnp.where(lane >= 32 * g, back_ref[base + (g - f) % PARTS], whole)
    if f:
        whole = pltpu.roll(whole, 128 - 32 * f, 1)
    if f == 2:
        inside = jnp.minimum(block, BLOCKS - 1)
        whole = whole * jnp.where(switch_ref[inside] == 1, PLASTIC, VISCOUS)
    all_ref[f, block] = whole


def near_kernel(covered_ref, back_ref, switch_ref, all_ref, index_ref):
    heavy = ranked(covered_ref, index_ref, BLOCKS) > 1
    blocks = [index_ref[r] for r in range(SLOTS)]
    for f in range(4):
        all_ref[f] = jnp.zeros(all_ref.shape[1:], F32)
        for r, block in enumerate(blocks):
            base = jnp.where(heavy, PARTS * r, PARTS * (SLOTS - 1))
            unpack(back_ref, switch_ref, all_ref, f, base, block)


def far_kernel(index_ref, far_ref, switch_ref, near_ref, gu_hbm, gs_hbm, gq_hbm, gf_hbm, all_ref, sems):
    copies = []
    for f, ref in ((0, gu_hbm), (1, gs_hbm), (3, gf_hbm), (2, gq_hbm)):
        for r in range(SLOTS, MOST):
            unpack(far_ref, switch_ref, all_ref, f, PARTS * (r - SLOTS), index_ref[r])
        copy = pltpu.make_async_copy(all_ref.at[f, pl.ds(0, BLOCKS)], ref, sems.at[f])
        copy.start()
        copies.append(copy)
    for copy in copies:
        copy.wait()


def shards(velocity, stress, thickness, forcing, switch, covered, reinit, cot_velocity, cot_stress, kernel):
    tile = (8, 128)

    def sds(*lead):
        return jax.ShapeDtypeStruct(lead + tile, F32)

    params = pltpu.CompilerParams(vmem_limit_bytes=12 * 1024 * 1024)
    own, send, keep = pl.pallas_call(
        gather_kernel,
        name="gather",
        out_shape=(sds(6 * SLOTS), sds(6 * SLOTS + 2), sds(3)),
        in_specs=[pl.BlockSpec(memory_space=pltpu.HBM)] * 9,
        out_specs=(vmem(), vmem(), vmem()),
        scratch_shapes=[pltpu.SMEM((BLOCKS,), jnp.int32)] * 2
        + [pltpu.VMEM((BLOCKS,) + tile, F32)] * 6
        + [pltpu.VMEM((BLOCKS,) + tile, jnp.int32), pltpu.SMEM((MOST + 1,), jnp.int32), pltpu.SemaphoreType.DMA((9,))],
        compiler_params=params,
    )(*[
        pltpu.with_memory_space_constraint(x, pltpu.HBM)
        for x in (covered, reinit, velocity, cot_velocity, stress, cot_stress, forcing, thickness, switch)
    ])
    got = lax.ppermute(send, "ocean", [(0, 1), (1, 0)])
    windows = jax.ShapeDtypeStruct((ICE, 24, 128), F32)
    packed, halves = pl.pallas_call(
        pack_own_kernel,
        name="pack_own",
        out_shape=(windows, jax.ShapeDtypeStruct((4, ROWS, ROWS), BF16)),
        in_specs=[vmem(), pl.BlockSpec(memory_space=pltpu.HBM)],
        out_specs=(vmem(), vmem()),
        scratch_shapes=[pltpu.VMEM((ROWS, ROWS), F32), pltpu.SemaphoreType.DMA],
        compiler_params=params,
    )(own, pltpu.with_memory_space_constraint(kernel, pltpu.HBM))
    packed, kept = pl.pallas_call(
        pack_got_kernel,
        name="pack_got",
        out_shape=(windows, sds()),
        in_specs=[vmem()] * 3,
        out_specs=(vmem(), vmem()),
        input_output_aliases={2: 0},
        compiler_params=params,
    )(got, keep, packed)
    arrived = lax.all_to_all(packed, "ice", split_axis=0, concat_axis=0, tiled=True)
    col = pltpu.VMEM((GROUPS,) + tile, F32)
    result = pl.pallas_call(
        work_kernel,
        name="work",
        out_shape=sds(ICE),
        in_specs=[vmem()] * 3,
        out_specs=vmem(),
        scratch_shapes=[col] * 7
        + [
            pltpu.VMEM((HALF, GROUPS) + tile, F32),
            pltpu.VMEM((2 * HALF,) + tile, F32),
            pltpu.VMEM((ROWS, 128), F32),
        ],
        compiler_params=params,
    )(arrived, halves, kept)
    back = lax.all_to_all(result, "ice", split_axis=0, concat_axis=0, tiled=True)
    far = lax.ppermute(back, "ocean", [(0, 1), (1, 0)])
    near, index = pl.pallas_call(
        near_kernel,
        name="near",
        out_shape=(sds(4, BLOCKS + 1), jax.ShapeDtypeStruct((MOST + 1,), jnp.int32)),
        in_specs=[smem(), vmem(), vmem()],
        out_specs=(vmem(), smem()),
        compiler_params=params,
    )(covered, back, switch)
    outs = pl.pallas_call(
        far_kernel,
        name="far",
        out_shape=(sds(BLOCKS),) * 4 + (sds(4, BLOCKS + 1),),
        in_specs=[smem()] + [vmem()] * 3,
        out_specs=(pl.BlockSpec(memory_space=pltpu.HBM),) * 4 + (vmem(),),
        scratch_shapes=[pltpu.SemaphoreType.DMA((4,))],
        input_output_aliases={3: 4},
        compiler_params=params,
    )(index, far, switch, near)
    return outs[:4]


def solution(mesh):
    cells = P("ocean", "ice", None)
    return jax.shard_map(
        shards,
        mesh=mesh,
        in_specs=(cells, cells, cells, cells, cells, P("ocean"), P("ocean"), cells, cells, P()),
        out_specs=(cells, cells, cells, cells),
        check_vma=False,
    )
```
